128 devices in a mesh: lat: 8 (over z, y_hi), lon: 16 (over y_lo, x, core).
Axes of the slice: x: 4, y: 4 (y_hi: 2, y_lo: 2; y = y_hi * 2 + y_lo), z: 4, core: 2. Of those that a mesh axis runs over, the one named last changes fastest.
Arguments:
- tokens: float32 [8, 16, 512, 1024], P('lat', 'lon')
- norm_gain: float32 [1024], replicated, may hold values from 0.5 to 6, as said below
- qkv_weight: bfloat16 [1024, 3072], replicated, may hold values from -0.1875 to 0.1875
- out_weight: bfloat16 [1024, 1024], replicated, may hold values from -0.1875 to 0.1875
- band_counts: int32 [8], P('lat'), may hold values from 256 to 512, as said below
- halo_rows: int32 [8, 2, 128], replicated, may hold values from 0 to 511, as said below
- window_mask: int32 [8, 16, 4, 5], P('lat', 'lon'), may hold values from 0 to 1, as said below
Outputs:
- updated: float32 [8, 16, 512, 1024], P('lat', 'lon')
The draws below stay inside these ranges and needn't reach their ends.
Inputs may be any that keep to these rules, and one draw needn't show every extreme that they name: `band_counts`: counts lie between 256 and 512; some band has exactly 512 and some band exactly 256. `halo_rows`: every entry names a live slot of the neighbour band it refers to (the band itself where that neighbour does not exist). `window_mask`: entries are 0 or 1; the middle entry (offset 0) is always 1. `norm_gain`: gains are positive.
All inputs are finite; a program needn't handle non-finite values.
Results may differ from the reference program's by a relative error of at most 0.002.
The reference program's roundings to bfloat16 on the way (of `normed`, `projected` and `attended`) count: a program that leaves them out, or rounds other values in their place, can miss the bound.
Values may be sent and summed in bfloat16 or wider, within the bound.
A program may use at most 192 MiB of HBM per device.

```python
import jax
import jax.numpy as jnp
from jax import lax

D = 1024
HEADS = 16
HEAD_DIM = 64
CAP = 512
QROWS = 128
REACH = 2
HALO = 128
NBANDS = 8
NSECT = 16
QBLK = 4


def shared_counts(key):
    folded = jax.random.fold_in(key, 11)
    first, second = jax.random.split(folded)
    counts = jax.random.randint(first, (NBANDS,), CAP // 2, CAP + 1)
    order = jax.random.permutation(second, NBANDS)
    counts = counts.at[order[0]].set(CAP).at[order[1]].set(CAP // 2)
    return counts.astype(jnp.int32)


def draw_band_counts(key, part):
    return shared_counts(key)


def draw_halo_rows(key, part):
    counts = shared_counts(key)
    band_ids = jnp.arange(NBANDS)
    north_counts = counts[jnp.maximum(band_ids - 1, 0)]
    south_counts = counts[jnp.minimum(band_ids + 1, NBANDS - 1)]
    offsets = jax.random.randint(jax.random.fold_in(key, 23), (NBANDS, 2, HALO), 0, 2 * HALO)
    offsets = offsets.at[:, :, 0].set(0)
    offsets = offsets.at[:, :, 1].set(2 * HALO - 1)
    edges = jnp.stack([north_counts, south_counts], axis=1)[:, :, None]
    return (edges - 1 - offsets).astype(jnp.int32)


def draw_window_mask(key, part):
    picks = jax.random.randint(jax.random.fold_in(key, 31), (NBANDS, NSECT, QBLK, 2 * REACH + 1), 0, 4)
    flags = (picks > 0).astype(jnp.int32)
    return flags.at[:, :, :, REACH].set(1)


def draw_tokens(key, part):
    shape = (NBANDS, NSECT, CAP, D)
    return jnp.clip(jax.random.normal(key, shape, jnp.float32), -6.0, 6.0)


def draw_norm_gain(key, part):
    return jax.random.uniform(key, (D,), jnp.float32, 0.5, 1.5)


def noise(own_key, dims, spread, bound, dtype=jnp.bfloat16):
    values = spread * jax.random.normal(own_key, dims, jnp.float32)
    return jnp.clip(values, min=-bound, max=bound).astype(dtype)


def setup_inputs(seed: int = 0) -> dict:
    key_of = jax.random.split(jax.random.key(seed), 8)
    return {
        "tokens": draw_tokens(jax.random.fold_in(key_of[7], 71), 0),
        "norm_gain": draw_norm_gain(jax.random.fold_in(key_of[7], 71), 0),
        "qkv_weight": noise(key_of[2], (D, 3 * D), D ** -0.5, 0.1875),
        "out_weight": noise(key_of[3], (D, D), D ** -0.5, 0.1875),
        "band_counts": draw_band_counts(jax.random.fold_in(key_of[7], 71), 0),
        "halo_rows": draw_halo_rows(jax.random.fold_in(key_of[7], 71), 0),
        "window_mask": draw_window_mask(jax.random.fold_in(key_of[7], 71), 0),
    }


epsilon = 1e-05

def normalize(values, gain):
    average = lax.optimization_barrier(jnp.mean(values, axis=-1, keepdims=True))
    centered = values - average
    variance = lax.optimization_barrier(jnp.mean(centered * centered, axis=-1, keepdims=True))
    return (centered * lax.rsqrt(variance + epsilon) * gain).astype(jnp.bfloat16)

def attend(queries, key_rows, allowed):
    query_heads = queries.astype(jnp.float32).reshape(CAP, HEADS, HEAD_DIM)
    key_heads = key_rows[:, :D].astype(jnp.float32).reshape(-1, HEADS, HEAD_DIM)
    value_heads = key_rows[:, D:].astype(jnp.float32).reshape(-1, HEADS, HEAD_DIM)
    scores = jnp.einsum('qhd,khd->hqk', query_heads, key_heads) * HEAD_DIM ** (-0.5)
    scores = jnp.where(allowed[None], scores, -jnp.inf)
    row_max = lax.optimization_barrier(jnp.max(scores, axis=-1, keepdims=True))
    weights = jnp.exp(scores - row_max)
    row_sum = lax.optimization_barrier(jnp.sum(weights, axis=-1, keepdims=True))
    rounded = lax.optimization_barrier(weights.astype(jnp.bfloat16))
    weighted = jnp.einsum('hqk,khd->hqd', rounded.astype(jnp.float32), value_heads)
    attended = (weighted / row_sum).transpose(1, 0, 2).reshape(CAP, D)
    return attended.astype(jnp.bfloat16)

def reference(tokens, norm_gain, qkv_weight, out_weight, band_counts, halo_rows, window_mask):
    normed = normalize(tokens, norm_gain)
    projected = jnp.dot(normed.reshape(-1, D), qkv_weight, preferred_element_type=jnp.float32).astype(jnp.bfloat16)
    projected = projected.reshape(NBANDS, NSECT, CAP, 3 * D)
    position = jnp.arange(CAP)

    def one_device(device_index):
        band_index = device_index // NSECT
        sector = device_index % NSECT
        key_valid = position < band_counts[band_index]
        row_flags = jnp.repeat(window_mask[band_index, sector] > 0, QROWS, axis=0)
        key_blocks = []
        allowed_blocks = []
        for offset in range(-REACH, REACH + 1):
            key_blocks.append(projected[band_index, (sector + offset) % NSECT, :, D:])
            allowed_blocks.append(row_flags[:, offset + REACH][:, None] & key_valid[None, :])
        north_band = jnp.maximum(band_index - 1, 0)
        south_band = jnp.minimum(band_index + 1, NBANDS - 1)
        key_blocks.append(projected[north_band, sector, :, D:][halo_rows[band_index, 0]])
        key_blocks.append(projected[south_band, sector, :, D:][halo_rows[band_index, 1]])
        allowed_blocks.append(jnp.broadcast_to(band_index > 0, (CAP, HALO)))
        allowed_blocks.append(jnp.broadcast_to(band_index < NBANDS - 1, (CAP, HALO)))
        key_rows = jnp.concatenate(key_blocks, axis=0)
        allowed = jnp.concatenate(allowed_blocks, axis=1)
        attended = attend(projected[band_index, sector, :, :D], key_rows, allowed)
        result = tokens[band_index, sector] + jnp.dot(attended, out_weight, preferred_element_type=jnp.float32)
        return jnp.where(key_valid[:, None], result, 0.0)
    results = lax.map(one_device, jnp.arange(NBANDS * NSECT))
    return results.reshape(NBANDS, NSECT, CAP, D)
```

```python
import functools

import jax
import jax.numpy as jnp
from jax import lax
from jax.experimental import pallas as pl
from jax.experimental.pallas import tpu as pltpu
from jax.sharding import PartitionSpec as P

HEADS = 16
EPS = 1e-05
BIG = 1e30
f32 = jnp.float32
bf16 = jnp.bfloat16
MESH = pl.DeviceIdType.MESH

OWN, PARTNER, NEAR, FAR, SHARED = range(5)


def layer_kernel(
    counts_ref, mask_ref, gain_ref, halo_ref, tokens_ref, wqkv_ref, wout_ref,
    out_ref,
    tok, wq, wo, nown, nrecv, hsend, hrecv, kbuf, vbuf, khalo, vhalo,
    q_ref, m_ref, acc_ref, qb_ref, ones_ref, hones_ref, att, row0,
    in_sem, w_sem, out_sem, send_sem, recv_sem,
):
    lat = lax.axis_index("lat")
    lon = lax.axis_index("lon")
    nlat = lax.axis_size("lat")
    nlon = lax.axis_size("lon")
    rows, width = tok.shape
    chunk = rows // 4
    halo = hsend.shape[1]
    side = 2 * lax.rem(lon, 2) - 1

    def wrap(x):
        return lax.rem(x + nlon, nlon)

    near = (lat, wrap(lon + side))
    far_to = (lat, wrap(lon - 2 * side))
    far_from = (lat, wrap(lon + 2 * side))
    partner = (lat, lon - side)
    south = (lax.rem(lat + 1, nlat), lon)
    north = (lax.rem(lat + nlat - 1, nlat), lon)

    def remote(src, dst, index, device):
        return pltpu.make_async_remote_copy(
            src_ref=src, dst_ref=dst, send_sem=send_sem.at[index], recv_sem=recv_sem.at[index],
            device_id=device, device_id_type=MESH,
        )

    send_near = remote(nown, nrecv.at[0], 0, near)
    send_far = remote(nown, nrecv.at[1], 1, far_to)
    send_south = remote(hsend.at[0], hrecv.at[pl.ds(0, halo)], 2, south)
    send_north = remote(hsend.at[1], hrecv.at[pl.ds(halo, halo)], 3, north)
    send_k = remote(kbuf.at[OWN], kbuf.at[PARTNER], 4, partner)
    send_v = remote(vbuf.at[OWN], vbuf.at[PARTNER], 5, partner)
    share_k = remote(kbuf.at[NEAR], kbuf.at[SHARED], 6, partner)
    share_v = remote(vbuf.at[NEAR], vbuf.at[SHARED], 7, partner)

    barrier = pltpu.get_barrier_semaphore()
    for device in (near, far_to, far_from, partner, south, north):
        pl.semaphore_signal(barrier, inc=1, device_id=device, device_id_type=MESH)

    tok_copies = []
    for r in range(4):
        part = pl.ds(r * chunk, chunk)
        copy = pltpu.make_async_copy(tokens_ref.at[part], tok.at[part], in_sem.at[r])
        copy.start()
        tok_copies.append(copy)
    w_copies = []
    for j in range(3):
        part = pl.ds(j * width, width)
        copy = pltpu.make_async_copy(wqkv_ref.at[:, part], wq.at[:, part], w_sem.at[j])
        copy.start()
        w_copies.append(copy)
    wo_copy = pltpu.make_async_copy(wout_ref, wo, w_sem.at[3])
    wo_copy.start()

    count = counts_ref[0]
    gain = gain_ref[...]

    for r in range(4):
        tok_copies[r].wait()
        x = tok[pl.ds(r * chunk, chunk), :]
        average = jnp.mean(x, axis=-1, keepdims=True)
        centered = x - average
        variance = jnp.mean(centered * centered, axis=-1, keepdims=True)
        y = centered * lax.rsqrt(variance + EPS) * gain
        if r == 0:
            row0[...] = jnp.broadcast_to(y[0:1, :], row0.shape)
        position = r * chunk + lax.broadcasted_iota(jnp.int32, (chunk, 1), 0)
        y = jnp.where(position < count, y, row0[0:1, :])
        nown[pl.ds(r * chunk, chunk), :] = y.astype(bf16)

    to_south = halo_ref[jnp.minimum(lat + 1, nlat - 1), 0:1, :]
    to_north = halo_ref[jnp.maximum(lat - 1, 0), 1:2, :]
    slot = lax.broadcasted_iota(jnp.int32, (rows, halo), 0)
    for j, wanted in ((0, to_south), (1, to_north)):
        pick = jnp.where(slot == wanted, 1.0, 0.0).astype(bf16)
        hsend[j] = lax.dot_general(
            pick, nown[...], (((0,), (0,)), ((), ())), preferred_element_type=f32
        ).astype(bf16)

    pl.semaphore_wait(barrier, 6)
    send_near.start()
    send_south.start()
    send_north.start()
    send_far.start()

    lane = lax.broadcasted_iota(jnp.int32, (1, 128), 1)
    low = lane < 64
    low_f = jnp.where(low, 1.0, 0.0)
    high_f = 1.0 - low_f
    position = lax.broadcasted_iota(jnp.int32, (rows, 1), 0)
    live = position < count
    live_f = jnp.where(live, 1.0, 0.0)
    ones_ref[0] = (live_f * high_f).astype(bf16)
    ones_ref[1] = (live_f * low_f).astype(bf16)
    has_north = jnp.where(lat > 0, 1.0, 0.0)
    has_south = jnp.where(lat < nlat - 1, 1.0, 0.0)
    hrow = lax.broadcasted_iota(jnp.int32, (2 * halo, 1), 0)
    hlive_f = jnp.where(hrow < halo, has_north, has_south)
    hones_ref[0] = (hlive_f * high_f).astype(bf16)
    hones_ref[1] = (hlive_f * low_f).astype(bf16)
    low_b = low_f.astype(bf16)
    high_b = high_f.astype(bf16)

    tile = width // 2

    def project_rows(src, column):
        cols = pl.ds(pl.multiple_of(column, tile), tile)
        return jnp.dot(src[...], wq[:, cols], preferred_element_type=f32)

    def project_k(src, dst):
        for t in range(2):
            dst[:, pl.ds(t * tile, tile)] = project_rows(src, width + t * tile).astype(bf16)

    def project_v(src, dst, alive):
        for t in range(2):
            v = project_rows(src, 2 * width + t * tile)
            dst[:, pl.ds(t * tile, tile)] = jnp.where(alive, v, 0.0).astype(bf16)

    def fill_bias(column):
        for r in range(4):
            seen = mask_ref[r, column].astype(f32)
            qb_ref[pl.ds(r * chunk, chunk), :] = jnp.full((chunk, 128), (1.0 - seen) * BIG, f32)

    def attend(k, v, ones, bias, first=False):
        keys = k.shape[0]
        group = 4

        def body(g, carry):
            for hh in range(group):
                h = g * group + hh
                odd = hh % 2
                cols = pl.ds(pl.multiple_of((g * (group // 2) + hh // 2) * 128, 128), 128)
                s = lax.dot_general(
                    q_ref[h], k[:, cols], (((1,), (1,)), ((), ())), preferred_element_type=f32
                )
                top = jnp.max(s, axis=1, keepdims=True)
                if bias:
                    top = top - qb_ref[...]
                if first:
                    new = jnp.broadcast_to(top, (rows, 128))
                else:
                    old = m_ref[h]
                    new = jnp.maximum(old, top)
                shift = new + qb_ref[...] if bias else new
                p = jnp.exp(s - jnp.tile(shift, (1, keys // 128))).astype(bf16)
                vh = v[:, cols] * (high_b if odd else low_b) + ones[odd]
                o = jnp.dot(p, vh, preferred_element_type=f32)
                if first:
                    acc_ref[h] = o
                else:
                    acc_ref[h] = acc_ref[h] * jnp.exp(old - new) + o
                m_ref[h] = new
            return carry

        lax.fori_loop(0, HEADS // group, body, 0)

    w_copies[0].wait()
    for t in range(2):
        q = project_rows(nown, t * tile) * 0.125
        for j in range(tile // 128):
            pair = q[:, j * 128:(j + 1) * 128]
            h = (t * (tile // 128) + j) * 2
            q_ref[h] = jnp.where(low, pair, 0.0).astype(bf16)
            q_ref[h + 1] = jnp.where(low, 0.0, pair).astype(bf16)
    w_copies[1].wait()
    project_k(nown, kbuf.at[OWN])
    send_k.start()
    w_copies[2].wait()
    project_v(nown, vbuf.at[OWN], live)
    send_v.start()
    attend(kbuf.at[OWN], vbuf.at[OWN], ones_ref, False, first=True)

    send_k.wait_recv()
    send_v.wait_recv()
    fill_bias(2 - side)
    attend(kbuf.at[PARTNER], vbuf.at[PARTNER], ones_ref, True)

    send_south.wait_recv()
    send_north.wait_recv()
    keep = hlive_f > 0.5
    hrecv[...] = jnp.where(keep, hrecv[...].astype(f32), row0[0:1, :]).astype(bf16)
    project_k(hrecv, khalo)
    project_v(hrecv, vhalo, keep)
    attend(khalo, vhalo, hones_ref, False)

    send_near.wait_recv()
    project_k(nrecv.at[0], kbuf.at[NEAR])
    share_k.start()
    project_v(nrecv.at[0], vbuf.at[NEAR], live)
    share_v.start()
    fill_bias(2 + side)
    attend(kbuf.at[NEAR], vbuf.at[NEAR], ones_ref, True)

    send_far.wait_recv()
    project_k(nrecv.at[1], kbuf.at[FAR])
    project_v(nrecv.at[1], vbuf.at[FAR], live)
    fill_bias(2 + 2 * side)
    attend(kbuf.at[FAR], vbuf.at[FAR], ones_ref, True)

    share_k.wait_recv()
    share_v.wait_recv()
    fill_bias(2 - 2 * side)
    attend(kbuf.at[SHARED], vbuf.at[SHARED], ones_ref, True)

    for j in range(HEADS // 2):
        even = acc_ref[2 * j]
        odd = acc_ref[2 * j + 1]
        value = jnp.where(low, even, odd)
        total = pltpu.roll(jnp.where(low, odd, even), 64, axis=1)
        att[:, j * 128:(j + 1) * 128] = (value / total).astype(bf16)
    wo_copy.wait()
    out_copies = []
    for r in range(4):
        part = pl.ds(r * chunk, chunk)
        y = tok[part, :] + jnp.dot(att[part, :], wo[...], preferred_element_type=f32)
        position = r * chunk + lax.broadcasted_iota(jnp.int32, (chunk, 1), 0)
        tok[part, :] = jnp.where(position < count, y, 0.0)
        copy = pltpu.make_async_copy(tok.at[part], out_ref.at[part], out_sem.at[r])
        copy.start()
        out_copies.append(copy)
    for copy in out_copies:
        copy.wait()
    for copy in (send_near, send_far, send_south, send_north, send_k, send_v, share_k, share_v):
        copy.wait_send()


def on_device(tokens, norm_gain, qkv_weight, out_weight, band_counts, halo_rows, window_mask):
    rows, width = tokens.shape[2:]
    halo = halo_rows.shape[2]
    vmem = pl.BlockSpec(memory_space=pltpu.VMEM)
    smem = pl.BlockSpec(memory_space=pltpu.SMEM)
    hbm = pl.BlockSpec(memory_space=pl.ANY)
    dma = pltpu.SemaphoreType.DMA
    out = pl.pallas_call(
        layer_kernel,
        out_shape=jax.ShapeDtypeStruct((rows, width), f32),
        in_specs=[smem, smem, vmem, vmem, hbm, hbm, hbm],
        out_specs=hbm,
        scratch_shapes=[
            pltpu.VMEM((rows, width), f32),
            pltpu.VMEM((width, 3 * width), bf16),
            pltpu.VMEM((width, width), bf16),
            pltpu.VMEM((rows, width), bf16),
            pltpu.VMEM((2, rows, width), bf16),
            pltpu.VMEM((2, halo, width), bf16),
            pltpu.VMEM((2 * halo, width), bf16),
            pltpu.VMEM((5, rows, width), bf16),
            pltpu.VMEM((5, rows, width), bf16),
            pltpu.VMEM((2 * halo, width), bf16),
            pltpu.VMEM((2 * halo, width), bf16),
            pltpu.VMEM((HEADS, rows, 128), bf16),
            pltpu.VMEM((HEADS, rows, 128), f32),
            pltpu.VMEM((HEADS, rows, 128), f32),
            pltpu.VMEM((rows, 128), f32),
            pltpu.VMEM((2, rows, 128), bf16),
            pltpu.VMEM((2, 2 * halo, 128), bf16),
            pltpu.VMEM((rows, width), bf16),
            pltpu.VMEM((8, width), f32),
            dma((4,)),
            dma((4,)),
            dma((4,)),
            dma((8,)),
            dma((8,)),
        ],
        compiler_params=pltpu.CompilerParams(
            collective_id=0, has_side_effects=True, vmem_limit_bytes=66_000_000
        ),
        name="layer",
    )(
        band_counts, window_mask[0, 0], norm_gain[None, :], halo_rows,
        tokens[0, 0], qkv_weight, out_weight,
    )
    return out[None, None]


def solution(mesh):
    in_specs = (
        P("lat", "lon", None, None),
        P(),
        P(),
        P(),
        P("lat"),
        P(),
        P("lat", "lon", None, None),
    )
    out_specs = P("lat", "lon", None, None)
    return jax.shard_map(
        on_device, mesh=mesh, in_specs=in_specs, out_specs=out_specs, check_vma=False
    )
```

```python
import jax
import jax.numpy as jnp
from jax import lax
from jax.experimental import pallas as pl
from jax.experimental.pallas import tpu as pltpu
from jax.sharding import PartitionSpec as P

HEADS = 16
EPS = 1e-05
BIG = 1e30
LIVE_LANE = 5
f32 = jnp.float32
bf16 = jnp.bfloat16
MESH = pl.DeviceIdType.MESH


def attention_kernel(
    counts_hbm, mask_hbm, gain_hbm, halo_hbm, tokens_ref, wqkv_ref,
    att_ref,
    counts_ref, mask_ref, gain_ref, halo_ref, tok, wq, nown, nrecv, hsend, hrecv, kbuf, vbuf, fk, fq, q_ref, m_ref, acc_ref,
    in_sem, w_sem, small_sem, send_sem, recv_sem,
):
    lat = lax.axis_index("lat")
    lon = lax.axis_index("lon")
    nlat = lax.axis_size("lat")
    nlon = lax.axis_size("lon")
    rows, width = tok.shape
    chunk = rows // 4
    half = rows // 2
    halo = hsend.shape[1]
    side = 2 * lax.rem(lon, 2) - 1

    def wrap(x):
        return lax.rem(x + nlon, nlon)

    partner_row = rows
    near_row = 2 * rows
    halo_row = near_row + rows
    far_row = halo_row + 2 * halo
    shared_row = far_row + rows

    near = (lat, wrap(lon + side))
    far_to = (lat, wrap(lon - 2 * side))
    far_from = (lat, wrap(lon + 2 * side))
    partner = (lat, lon - side)
    south = (lax.rem(lat + 1, nlat), lon)
    north = (lax.rem(lat + nlat - 1, nlat), lon)

    def remote(src, dst, index, device):
        return pltpu.make_async_remote_copy(
            src_ref=src, dst_ref=dst, send_sem=send_sem.at[index], recv_sem=recv_sem.at[index],
            device_id=device, device_id_type=MESH,
        )

    halves = (pl.ds(0, half), pl.ds(half, half))
    send_near = [remote(nown.at[p], nrecv.at[0, p], j, near) for j, p in enumerate(halves)]
    send_far = [remote(nown.at[p], nrecv.at[1, p], 2 + j, far_to) for j, p in enumerate(halves)]
    send_south = remote(hsend.at[0], hrecv.at[pl.ds(0, halo)], 4, south)
    send_north = remote(hsend.at[1], hrecv.at[pl.ds(halo, halo)], 5, north)
    own = pl.ds(0, rows)
    send_k = remote(kbuf.at[own], kbuf.at[pl.ds(partner_row, rows)], 6, partner)
    send_v = remote(vbuf.at[own], vbuf.at[pl.ds(partner_row, rows)], 7, partner)
    here = pl.ds(near_row, rows)
    there = pl.ds(shared_row, rows)
    share_k = remote(kbuf.at[here], kbuf.at[there], 8, partner)
    share_v = remote(vbuf.at[here], vbuf.at[there], 9, partner)

    small_copies = [
        pltpu.make_async_copy(src, dst, small_sem.at[j])
        for j, (src, dst) in enumerate((
            (gain_hbm, gain_ref), (halo_hbm, halo_ref), (counts_hbm, counts_ref),
            (mask_hbm, mask_ref),
        ))
    ]
    small_copies[0].start()
    tok_copies = []
    for r in range(4):
        part = pl.ds(r * chunk, chunk)
        copy = pltpu.make_async_copy(tokens_ref.at[part], tok.at[part], in_sem.at[r])
        copy.start()
        tok_copies.append(copy)
    for copy in small_copies[1:]:
        copy.start()
    w_copies = []
    for j in range(3):
        part = pl.ds(j * width, width)
        w_copies.append(
            pltpu.make_async_copy(wqkv_ref.at[:, part], wq.at[:, part], w_sem.at[j])
        )

    barrier = pltpu.get_barrier_semaphore()
    for device in (near, far_to, far_from, partner, south, north):
        pl.semaphore_signal(barrier, inc=1, device_id=device, device_id_type=MESH)

    small_copies[0].wait()
    gain = gain_ref[...]
    for r in range(4):
        part = pl.ds(r * chunk, chunk)
        tok_copies[r].wait()
        if r > 0:
            w_copies[r - 1].start()
        x = tok[part, :]
        average = jnp.mean(x, axis=-1, keepdims=True)
        centered = x - average
        variance = jnp.mean(centered * centered, axis=-1, keepdims=True)
        nown[part, :] = (centered * lax.rsqrt(variance + EPS) * gain).astype(bf16)
        if r == 1:
            pl.semaphore_wait(barrier, 6)
            send_near[0].start()
    send_near[1].start()
    for copy in small_copies[1:]:
        copy.wait()

    to_south = halo_ref[jnp.minimum(lat + 1, nlat - 1), 0:1, :]
    to_north = halo_ref[jnp.maximum(lat - 1, 0), 1:2, :]
    slot = lax.broadcasted_iota(jnp.int32, (rows, halo), 0)
    for j, wanted in ((0, to_south), (1, to_north)):
        pick = jnp.where(slot == wanted, 1.0, 0.0).astype(bf16)
        hsend[j] = lax.dot_general(
            pick, nown[...], (((0,), (0,)), ((), ())), preferred_element_type=f32
        ).astype(bf16)

    @pl.when(lat == 0)
    def _():
        hrecv[pl.ds(0, halo), :] = jnp.zeros((halo, width), bf16)

    @pl.when(lat == nlat - 1)
    def _():
        hrecv[pl.ds(halo, halo), :] = jnp.zeros((halo, width), bf16)

    count = counts_ref[0]
    lane = lax.broadcasted_iota(jnp.int32, (1, 128), 1)
    low = lane < 64
    for r in range(4):
        feature = jnp.where(lane == LIVE_LANE, 1.0, 0.0)
        for c in range(5):
            hidden = (mask_ref[r, c].astype(f32) - 1.0) * BIG
            feature = feature + jnp.where(lane == c, hidden, 0.0)
        fq[pl.ds(r * chunk, chunk), :] = jnp.broadcast_to(feature, (chunk, 128)).astype(bf16)
    lanes = lax.broadcasted_iota(jnp.int32, (rows, 128), 1)
    position = lax.broadcasted_iota(jnp.int32, (rows, 128), 0)
    dead = jnp.where((lanes == LIVE_LANE) & (position >= count), -BIG, 0.0)
    for row, hops in (
        (0, 0), (partner_row, -side), (near_row, side), (far_row, 2 * side),
        (shared_row, -2 * side),
    ):
        fk[pl.ds(row, rows), :] = jnp.where(lanes == 2 + hops, 1.0, dead).astype(bf16)
    hlanes = lax.broadcasted_iota(jnp.int32, (2 * halo, 128), 1)
    hposition = lax.broadcasted_iota(jnp.int32, (2 * halo, 128), 0)
    gone = jnp.where(
        hposition < halo, jnp.where(lat == 0, -BIG, 0.0), jnp.where(lat == nlat - 1, -BIG, 0.0)
    )
    fk[pl.ds(halo_row, 2 * halo), :] = jnp.where(hlanes == LIVE_LANE, gone, 0.0).astype(bf16)

    low_b = jnp.where(low, 1.0, 0.0).astype(bf16)
    high_b = jnp.where(low, 0.0, 1.0).astype(bf16)

    tile = width // 2

    def project(src, column):
        return jnp.dot(src, wq[:, pl.ds(column, tile)], preferred_element_type=f32)

    def project_to(dst, row, src, column):
        for t in range(2):
            dst[pl.ds(row, src.shape[0]), pl.ds(t * tile, tile)] = project(
                src[...], column + t * tile
            ).astype(bf16)

    def attend(row, keys, first=False, last=False, middle=None):
        group = 4
        part = pl.ds(row, keys)

        def body(g, carry):
            if middle is not None:
                pl.when(g == 1)(middle)
            done = []
            for hh in range(group):
                h = g * group + hh
                odd = hh % 2
                cols = pl.ds(pl.multiple_of((g * (group // 2) + hh // 2) * 128, 128), 128)
                s = lax.dot_general(
                    jnp.concatenate([q_ref[h], fq[...]], axis=1),
                    jnp.concatenate([kbuf[part, cols], fk[part, :]], axis=1),
                    (((1,), (1,)), ((), ())), preferred_element_type=f32,
                )
                new = jnp.max(s, axis=1, keepdims=True)
                if first:
                    new = jnp.broadcast_to(new, (rows, 128))
                else:
                    old = m_ref[h]
                    new = jnp.maximum(old, new)
                p = jnp.exp(s - jnp.tile(new, (1, keys // 128))).astype(bf16)
                mine, other = (high_b, low_b) if odd else (low_b, high_b)
                o = jnp.dot(p, vbuf[part, cols] * mine + other, preferred_element_type=f32)
                if not first:
                    o = acc_ref[h] * jnp.exp(old - new) + o
                if last:
                    done.append(o)
                    if odd:
                        value = jnp.where(low, done[-2], done[-1])
                        total = pltpu.roll(jnp.where(low, done[-1], done[-2]), 64, axis=1)
                        att_ref[:, cols] = (value / total).astype(bf16)
                else:
                    acc_ref[h] = o
                    m_ref[h] = new
            return carry

        lax.fori_loop(0, HEADS // group, body, 0)

    def start_rest():
        pl.when(lat < nlat - 1)(send_south.start)
        pl.when(lat > 0)(send_north.start)
        for copy in send_far:
            copy.start()

    w_copies[0].wait()
    for t in range(2):
        q = project(nown[...], t * tile) * 0.125
        for j in range(tile // 128):
            pair = q[:, j * 128:(j + 1) * 128]
            h = (t * (tile // 128) + j) * 2
            q_ref[h] = jnp.where(low, pair, 0.0).astype(bf16)
            q_ref[h + 1] = jnp.where(low, 0.0, pair).astype(bf16)
    w_copies[1].wait()
    project_to(kbuf, 0, nown, width)
    send_k.start()
    w_copies[2].wait()
    project_to(vbuf, 0, nown, 2 * width)
    send_v.start()

    send_k.wait_recv()
    send_v.wait_recv()
    attend(0, 2 * rows, first=True, middle=start_rest)

    for copy in send_near:
        copy.wait_recv()
    project_to(kbuf, near_row, nrecv.at[0], width)
    share_k.start()
    project_to(vbuf, near_row, nrecv.at[0], 2 * width)
    share_v.start()
    attend(near_row, rows)

    pl.when(lat > 0)(send_south.wait_recv)
    pl.when(lat < nlat - 1)(send_north.wait_recv)
    project_to(kbuf, halo_row, hrecv, width)
    project_to(vbuf, halo_row, hrecv, 2 * width)
    for j, p in enumerate(halves):
        send_far[j].wait_recv()
        row = far_row + j * half
        project_to(kbuf, row, nrecv.at[1, p], width)
        project_to(vbuf, row, nrecv.at[1, p], 2 * width)
    share_k.wait_recv()
    share_v.wait_recv()
    attend(halo_row, 2 * halo + 2 * rows, last=True)

    for copy in (*send_near, *send_far, send_k, send_v, share_k, share_v):
        copy.wait_send()

    pl.when(lat < nlat - 1)(send_south.wait_send)
    pl.when(lat > 0)(send_north.wait_send)


def output_kernel(counts_ref, att_ref, tokens_ref, wout_ref, out_ref):
    chunk = out_ref.shape[0]
    y = tokens_ref[...] + jnp.dot(att_ref[...], wout_ref[...], preferred_element_type=f32)
    position = pl.program_id(0) * chunk + lax.broadcasted_iota(jnp.int32, (chunk, 1), 0)
    out_ref[...] = jnp.where(position < counts_ref[0], y, 0.0)


def on_device(tokens, norm_gain, qkv_weight, out_weight, band_counts, halo_rows, window_mask):
    rows, width = tokens.shape[2:]
    halo = halo_rows.shape[2]
    vmem = pl.BlockSpec(memory_space=pltpu.VMEM)
    smem = pl.BlockSpec(memory_space=pltpu.SMEM)
    hbm = pl.BlockSpec(memory_space=pltpu.MemorySpace.HBM)
    dma = pltpu.SemaphoreType.DMA
    keys = 5 * rows + 2 * halo
    att = pl.pallas_call(
        attention_kernel,
        out_shape=jax.ShapeDtypeStruct((rows, width), bf16),
        in_specs=[hbm] * 6,
        out_specs=vmem,
        scratch_shapes=[
            pltpu.SMEM(band_counts.shape, jnp.int32),
            pltpu.SMEM(window_mask.shape[2:], jnp.int32),
            pltpu.VMEM((1, width), f32),
            pltpu.VMEM(halo_rows.shape, jnp.int32),
            pltpu.VMEM((rows, width), f32),
            pltpu.VMEM((width, 3 * width), bf16),
            pltpu.VMEM((rows, width), bf16),
            pltpu.VMEM((2, rows, width), bf16),
            pltpu.VMEM((2, halo, width), bf16),
            pltpu.VMEM((2 * halo, width), bf16),
            pltpu.VMEM((keys, width), bf16),
            pltpu.VMEM((keys, width), bf16),
            pltpu.VMEM((keys, 128), bf16),
            pltpu.VMEM((rows, 128), bf16),
            pltpu.VMEM((HEADS, rows, 128), bf16),
            pltpu.VMEM((HEADS, rows, 128), f32),
            pltpu.VMEM((HEADS, rows, 128), f32),
            dma((4,)),
            dma((3,)),
            dma((4,)),
            dma((10,)),
            dma((10,)),
        ],
        compiler_params=pltpu.CompilerParams(
            collective_id=0, has_side_effects=True, vmem_limit_bytes=56_000_000
        ),
        name="attention",
    )(
        band_counts, window_mask[0, 0], norm_gain[None, :], halo_rows,
        tokens[0, 0], qkv_weight,
    )
    chunk = rows // 4
    out = pl.pallas_call(
        output_kernel,
        out_shape=jax.ShapeDtypeStruct((rows, width), f32),
        grid=(4,),
        in_specs=[
            smem,
            pl.BlockSpec((chunk, width), lambda i: (i, 0)),
            pl.BlockSpec((chunk, width), lambda i: (i, 0)),
            vmem,
        ],
        out_specs=pl.BlockSpec((chunk, width), lambda i: (i, 0)),
        compiler_params=pltpu.CompilerParams(vmem_limit_bytes=20_000_000),
        name="output",
    )(band_counts, att, tokens[0, 0], out_weight)
    return out[None, None]


def solution(mesh):
    in_specs = (
        P("lat", "lon", None, None),
        P(),
        P(),
        P(),
        P("lat"),
        P(),
        P("lat", "lon", None, None),
    )
    out_specs = P("lat", "lon", None, None)
    return jax.shard_map(
        on_device, mesh=mesh, in_specs=in_specs, out_specs=out_specs, check_vma=False
    )
```

```python
import jax
import jax.numpy as jnp
from jax import lax
from jax.experimental import pallas as pl
from jax.experimental.pallas import tpu as pltpu
from jax.sharding import PartitionSpec as P

HEADS = 16
EPS = 1e-05
BIG = 1e30
LIVE_LANE = 5
f32 = jnp.float32
bf16 = jnp.bfloat16
MESH = pl.DeviceIdType.MESH


def attention_kernel(
    counts_hbm, mask_hbm, gain_hbm, halo_hbm, tokens_ref, wqkv_ref,
    att_ref,
    counts_ref, mask_ref, gain_ref, halo_ref, tok, wq, nown, nrecv, hsend, hrecv, kbuf, vbuf, fk, fq, q_ref, m_ref, acc_ref, att,
    in_sem, w_sem, small_sem, att_sem, send_sem, recv_sem,
):
    lat = lax.axis_index("lat")
    lon = lax.axis_index("lon")
    nlat = lax.axis_size("lat")
    nlon = lax.axis_size("lon")
    rows, width = tok.shape
    chunk = rows // 4
    half = rows // 2
    halo = hsend.shape[1]
    side = 2 * lax.rem(lon, 2) - 1

    def wrap(x):
        return lax.rem(x + nlon, nlon)

    partner_row = rows
    near_row = 2 * rows
    shared_row = near_row + rows
    halo_row = shared_row + rows
    far_row = halo_row + 2 * halo

    near = (lat, wrap(lon + side))
    far_to = (lat, wrap(lon - 2 * side))
    far_from = (lat, wrap(lon + 2 * side))
    partner = (lat, lon - side)
    south = (lax.rem(lat + 1, nlat), lon)
    north = (lax.rem(lat + nlat - 1, nlat), lon)

    def remote(src, dst, index, device):
        return pltpu.make_async_remote_copy(
            src_ref=src, dst_ref=dst, send_sem=send_sem.at[index], recv_sem=recv_sem.at[index],
            device_id=device, device_id_type=MESH,
        )

    halves = (pl.ds(0, half), pl.ds(half, half))
    send_near = [remote(nown.at[p], nrecv.at[0, p], j, near) for j, p in enumerate(halves)]
    send_far = [remote(nown.at[p], nrecv.at[1, p], 2 + j, far_to) for j, p in enumerate(halves)]
    send_south = remote(hsend.at[0], hrecv.at[pl.ds(0, halo)], 4, south)
    send_north = remote(hsend.at[1], hrecv.at[pl.ds(halo, halo)], 5, north)
    own = pl.ds(0, rows)
    send_k = remote(kbuf.at[own], kbuf.at[pl.ds(partner_row, rows)], 6, partner)
    send_v = remote(vbuf.at[own], vbuf.at[pl.ds(partner_row, rows)], 7, partner)
    here = pl.ds(near_row, rows)
    there = pl.ds(shared_row, rows)
    share_k = remote(kbuf.at[here], kbuf.at[there], 8, partner)
    share_v = remote(vbuf.at[here], vbuf.at[there], 9, partner)

    small_copies = [
        pltpu.make_async_copy(src, dst, small_sem.at[j])
        for j, (src, dst) in enumerate((
            (gain_hbm, gain_ref), (halo_hbm, halo_ref), (counts_hbm, counts_ref),
            (mask_hbm, mask_ref),
        ))
    ]
    small_copies[0].start()
    tok_copies = []
    for r in range(4):
        part = pl.ds(r * chunk, chunk)
        copy = pltpu.make_async_copy(tokens_ref.at[part], tok.at[part], in_sem.at[r])
        copy.start()
        tok_copies.append(copy)
    for copy in small_copies[1:]:
        copy.start()
    w_copies = []
    for j in range(3):
        part = pl.ds(j * width, width)
        w_copies.append(
            pltpu.make_async_copy(wqkv_ref.at[:, part], wq.at[:, part], w_sem.at[j])
        )

    barrier = pltpu.get_barrier_semaphore()

    def greet(device):
        pl.semaphore_signal(barrier, inc=1, device_id=device, device_id_type=MESH)

    for device in (near, far_to, far_from, partner):
        greet(device)

    @pl.when(lat < nlat - 1)
    def _():
        greet(south)

    @pl.when(lat > 0)
    def _():
        greet(north)

    greeted = 4 + jnp.where(lat < nlat - 1, 1, 0) + jnp.where(lat > 0, 1, 0)

    small_copies[0].wait()
    gain = gain_ref[...]
    for r in range(4):
        part = pl.ds(r * chunk, chunk)
        tok_copies[r].wait()
        if r > 0:
            w_copies[r - 1].start()
        x = tok[part, :]
        average = jnp.mean(x, axis=-1, keepdims=True)
        centered = x - average
        variance = jnp.mean(centered * centered, axis=-1, keepdims=True)
        nown[part, :] = (centered * lax.rsqrt(variance + EPS) * gain).astype(bf16)
        if r == 1:
            pl.semaphore_wait(barrier, greeted)
            send_near[0].start()
    send_near[1].start()
    for copy in small_copies[1:]:
        copy.wait()

    to_south = halo_ref[jnp.minimum(lat + 1, nlat - 1), 0:1, :]
    to_north = halo_ref[jnp.maximum(lat - 1, 0), 1:2, :]
    slot = lax.broadcasted_iota(jnp.int32, (rows, halo), 0)
    for j, wanted in ((0, to_south), (1, to_north)):
        pick = jnp.where(slot == wanted, 1.0, 0.0).astype(bf16)
        hsend[j] = lax.dot_general(
            pick, nown[...], (((0,), (0,)), ((), ())), preferred_element_type=f32
        ).astype(bf16)

    @pl.when(lat == 0)
    def _():
        hrecv[pl.ds(0, halo), :] = jnp.zeros((halo, width), bf16)

    @pl.when(lat == nlat - 1)
    def _():
        hrecv[pl.ds(halo, halo), :] = jnp.zeros((halo, width), bf16)

    count = counts_ref[0]
    lane = lax.broadcasted_iota(jnp.int32, (1, 128), 1)
    low = lane < 64
    for r in range(4):
        feature = jnp.where(lane == LIVE_LANE, 1.0, 0.0)
        for c in range(5):
            hidden = (mask_ref[r, c].astype(f32) - 1.0) * BIG
            feature = feature + jnp.where(lane == c, hidden, 0.0)
        fq[pl.ds(r * chunk, chunk), :] = jnp.broadcast_to(feature, (chunk, 128)).astype(bf16)
    lanes = lax.broadcasted_iota(jnp.int32, (rows, 128), 1)
    position = lax.broadcasted_iota(jnp.int32, (rows, 128), 0)
    dead = jnp.where((lanes == LIVE_LANE) & (position >= count), -BIG, 0.0)
    for row, hops in (
        (0, 0), (partner_row, -side), (near_row, side), (far_row, 2 * side),
        (shared_row, -2 * side),
    ):
        fk[pl.ds(row, rows), :] = jnp.where(lanes == 2 + hops, 1.0, dead).astype(bf16)
    hlanes = lax.broadcasted_iota(jnp.int32, (2 * halo, 128), 1)
    hposition = lax.broadcasted_iota(jnp.int32, (2 * halo, 128), 0)
    gone = jnp.where(
        hposition < halo, jnp.where(lat == 0, -BIG, 0.0), jnp.where(lat == nlat - 1, -BIG, 0.0)
    )
    fk[pl.ds(halo_row, 2 * halo), :] = jnp.where(hlanes == LIVE_LANE, gone, 0.0).astype(bf16)

    low_b = jnp.where(low, 1.0, 0.0).astype(bf16)
    high_b = jnp.where(low, 0.0, 1.0).astype(bf16)

    tile = width // 2

    def project(src, column):
        return jnp.dot(src, wq[:, pl.ds(column, tile)], preferred_element_type=f32)

    def project_to(dst, row, src, column):
        for t in range(2):
            dst[pl.ds(row, src.shape[0]), pl.ds(t * tile, tile)] = project(
                src[...], column + t * tile
            ).astype(bf16)

    def att_copy(g):
        cols = pl.ds(pl.multiple_of(g * 256, 256), 256)
        return pltpu.make_async_copy(att.at[g], att_ref.at[:, cols], att_sem.at[g])

    def attend(row, keys, first=False, last=False, between=()):
        group = 4
        part = pl.ds(row, keys)

        def body(g, carry):
            for n, action in enumerate(between):
                pl.when(g == n + 1)(action)
            done = []
            for hh in range(group):
                h = g * group + hh
                odd = hh % 2
                cols = pl.ds(pl.multiple_of((g * (group // 2) + hh // 2) * 128, 128), 128)
                s = lax.dot_general(
                    jnp.concatenate([q_ref[h], fq[...]], axis=1),
                    jnp.concatenate([kbuf[part, cols], fk[part, :]], axis=1),
                    (((1,), (1,)), ((), ())), preferred_element_type=f32,
                )
                new = jnp.max(s, axis=1, keepdims=True)
                if first:
                    new = jnp.broadcast_to(new, (rows, 128))
                else:
                    old = m_ref[h]
                    new = jnp.maximum(old, new)
                p = jnp.exp(s - jnp.tile(new, (1, keys // 128))).astype(bf16)
                mine, other = (high_b, low_b) if odd else (low_b, high_b)
                o = jnp.dot(p, vbuf[part, cols] * mine + other, preferred_element_type=f32)
                if not first:
                    o = acc_ref[h] * jnp.exp(old - new) + o
                if last:
                    done.append(o)
                    if odd:
                        value = jnp.where(low, done[-2], done[-1])
                        total = pltpu.roll(jnp.where(low, done[-1], done[-2]), 64, axis=1)
                        att[g, :, (hh // 2) * 128:(hh // 2 + 1) * 128] = (value / total).astype(bf16)
                else:
                    acc_ref[h] = o
                    m_ref[h] = new
            if last:
                att_copy(g).start()
            return carry

        lax.fori_loop(0, HEADS // group, body, 0)

    def start_rest():
        pl.when(lat < nlat - 1)(send_south.start)
        pl.when(lat > 0)(send_north.start)
        for copy in send_far:
            copy.start()

    def share_near():
        for copy in send_near:
            copy.wait_recv()
        project_to(kbuf, near_row, nrecv.at[0], width)
        share_k.start()
        project_to(vbuf, near_row, nrecv.at[0], 2 * width)
        share_v.start()

    w_copies[0].wait()
    for t in range(2):
        q = project(nown[...], t * tile) * 0.125
        for j in range(tile // 128):
            pair = q[:, j * 128:(j + 1) * 128]
            h = (t * (tile // 128) + j) * 2
            q_ref[h] = jnp.where(low, pair, 0.0).astype(bf16)
            q_ref[h + 1] = jnp.where(low, 0.0, pair).astype(bf16)
    w_copies[1].wait()
    project_to(kbuf, 0, nown, width)
    send_k.start()
    w_copies[2].wait()
    project_to(vbuf, 0, nown, 2 * width)
    send_v.start()

    send_k.wait_recv()
    send_v.wait_recv()
    attend(0, 2 * rows, first=True, between=(start_rest, share_near))

    share_k.wait_recv()
    share_v.wait_recv()
    attend(near_row, 2 * rows)

    pl.when(lat > 0)(send_south.wait_recv)
    pl.when(lat < nlat - 1)(send_north.wait_recv)
    project_to(kbuf, halo_row, hrecv, width)
    project_to(vbuf, halo_row, hrecv, 2 * width)
    for j, p in enumerate(halves):
        send_far[j].wait_recv()
        row = far_row + j * half
        project_to(kbuf, row, nrecv.at[1, p], width)
        project_to(vbuf, row, nrecv.at[1, p], 2 * width)
    attend(halo_row, 2 * halo + rows, last=True)
    for g in range(HEADS // 4):
        att_copy(g).wait()

    for copy in (*send_near, *send_far, send_k, send_v, share_k, share_v):
        copy.wait_send()

    pl.when(lat < nlat - 1)(send_south.wait_send)
    pl.when(lat > 0)(send_north.wait_send)


def output_kernel(
    counts_ref, att_hbm, tokens_hbm, wout_hbm, out_hbm, att, tok, wo, out, in_sem, w_sem, out_sem
):
    rows, width = tok.shape
    tiles = w_sem.shape[0]
    parts = [pl.ds(j * (width // tiles), width // tiles) for j in range(tiles)]
    att_copy = pltpu.make_async_copy(att_hbm, att, in_sem.at[tiles])
    att_copy.start()
    w_copies = []
    tok_copies = []
    for j, p in enumerate(parts):
        w_copies.append(pltpu.make_async_copy(wout_hbm.at[:, p], wo.at[:, p], w_sem.at[j]))
        w_copies[j].start()
        tok_copies.append(pltpu.make_async_copy(tokens_hbm.at[:, p], tok.at[:, p], in_sem.at[j]))
        tok_copies[j].start()
    live = lax.broadcasted_iota(jnp.int32, (rows, 1), 0) < counts_ref[0]
    att_copy.wait()
    out_copies = []
    for j, p in enumerate(parts):
        w_copies[j].wait()
        tok_copies[j].wait()
        y = tok[:, p] + jnp.dot(att[...], wo[:, p], preferred_element_type=f32)
        out[:, p] = jnp.where(live, y, 0.0)
        out_copies.append(pltpu.make_async_copy(out.at[:, p], out_hbm.at[:, p], out_sem.at[j]))
        out_copies[j].start()
    for copy in out_copies:
        copy.wait()


def on_device(tokens, norm_gain, qkv_weight, out_weight, band_counts, halo_rows, window_mask):
    rows, width = tokens.shape[2:]
    halo = halo_rows.shape[2]
    smem = pl.BlockSpec(memory_space=pltpu.SMEM)
    hbm = pl.BlockSpec(memory_space=pltpu.MemorySpace.HBM)
    dma = pltpu.SemaphoreType.DMA
    keys = 5 * rows + 2 * halo
    att = pl.pallas_call(
        attention_kernel,
        out_shape=jax.ShapeDtypeStruct((rows, width), bf16),
        in_specs=[hbm] * 6,
        out_specs=hbm,
        scratch_shapes=[
            pltpu.SMEM(band_counts.shape, jnp.int32),
            pltpu.SMEM(window_mask.shape[2:], jnp.int32),
            pltpu.VMEM((1, width), f32),
            pltpu.VMEM(halo_rows.shape, jnp.int32),
            pltpu.VMEM((rows, width), f32),
            pltpu.VMEM((width, 3 * width), bf16),
            pltpu.VMEM((rows, width), bf16),
            pltpu.VMEM((2, rows, width), bf16),
            pltpu.VMEM((2, halo, width), bf16),
            pltpu.VMEM((2 * halo, width), bf16),
            pltpu.VMEM((keys, width), bf16),
            pltpu.VMEM((keys, width), bf16),
            pltpu.VMEM((keys, 128), bf16),
            pltpu.VMEM((rows, 128), bf16),
            pltpu.VMEM((HEADS, rows, 128), bf16),
            pltpu.VMEM((HEADS, rows, 128), f32),
            pltpu.VMEM((HEADS, rows, 128), f32),
            pltpu.VMEM((HEADS // 4, rows, 256), bf16),
            dma((4,)),
            dma((3,)),
            dma((4,)),
            dma((HEADS // 4,)),
            dma((10,)),
            dma((10,)),
        ],
        compiler_params=pltpu.CompilerParams(
            collective_id=0, has_side_effects=True, vmem_limit_bytes=67_000_000
        ),
        name="attention",
    )(
        band_counts, window_mask[0, 0], norm_gain[None, :], halo_rows,
        tokens[0, 0], qkv_weight,
    )
    out = pl.pallas_call(
        output_kernel,
        out_shape=jax.ShapeDtypeStruct((rows, width), f32),
        in_specs=[smem, hbm, hbm, hbm],
        out_specs=hbm,
        scratch_shapes=[
            pltpu.VMEM((rows, width), bf16),
            pltpu.VMEM((rows, width), f32),
            pltpu.VMEM((width, width), bf16),
            pltpu.VMEM((rows, width), f32),
            dma((5,)),
            dma((4,)),
            dma((4,)),
        ],
        compiler_params=pltpu.CompilerParams(vmem_limit_bytes=67_000_000),
        name="output",
    )(band_counts, att, tokens[0, 0], out_weight)
    return out[None, None]


def solution(mesh):
    in_specs = (
        P("lat", "lon", None, None),
        P(),
        P(),
        P(),
        P("lat"),
        P(),
        P("lat", "lon", None, None),
    )
    out_specs = P("lat", "lon", None, None)
    return jax.shard_map(
        on_device, mesh=mesh, in_specs=in_specs, out_specs=out_specs, check_vma=False
    )
```

```python
import jax
import jax.numpy as jnp
from jax import lax
from jax.experimental import pallas as pl
from jax.experimental.pallas import tpu as pltpu
from jax.sharding import PartitionSpec as P

HEADS = 16
EPS = 1e-05
BIG = 1e30
LIVE_LANE = 5
f32 = jnp.float32
bf16 = jnp.bfloat16
MESH = pl.DeviceIdType.MESH


def attention_kernel(
    counts_hbm, mask_hbm, gain_hbm, halo_hbm, tokens_ref, wqkv_ref,
    att_ref,
    counts_ref, mask_ref, gain_ref, halo_ref, tok, wq, nown, nrecv, hsend, hrecv, kbuf, vbuf, fk, fq, q_ref, m_ref, acc_ref, att, sbuf,
    in_sem, w_sem, small_sem, att_sem, send_sem, recv_sem,
):
    lat = lax.axis_index("lat")
    lon = lax.axis_index("lon")
    nlat = lax.axis_size("lat")
    nlon = lax.axis_size("lon")
    rows, width = tok.shape
    chunk = rows // 4
    half = rows // 2
    halo = hsend.shape[1]
    side = 2 * lax.rem(lon, 2) - 1

    def wrap(x):
        return lax.rem(x + nlon, nlon)

    partner_row = rows
    near_row = 2 * rows
    shared_row = near_row + rows
    halo_row = shared_row + rows
    far_row = halo_row + 2 * halo

    near = (lat, wrap(lon + side))
    far_to = (lat, wrap(lon - 2 * side))
    far_from = (lat, wrap(lon + 2 * side))
    partner = (lat, lon - side)
    south = (lax.rem(lat + 1, nlat), lon)
    north = (lax.rem(lat + nlat - 1, nlat), lon)

    def remote(src, dst, index, device):
        return pltpu.make_async_remote_copy(
            src_ref=src, dst_ref=dst, send_sem=send_sem.at[index], recv_sem=recv_sem.at[index],
            device_id=device, device_id_type=MESH,
        )

    halves = (pl.ds(0, half), pl.ds(half, half))
    send_near = [remote(nown.at[p], nrecv.at[0, p], j, near) for j, p in enumerate(halves)]
    send_far = [remote(nown.at[p], nrecv.at[1, p], 2 + j, far_to) for j, p in enumerate(halves)]
    send_south = remote(hsend.at[0], hrecv.at[pl.ds(0, halo)], 4, south)
    send_north = remote(hsend.at[1], hrecv.at[pl.ds(halo, halo)], 5, north)
    own = pl.ds(0, rows)
    send_k = remote(kbuf.at[own], kbuf.at[pl.ds(partner_row, rows)], 6, partner)
    send_v = remote(vbuf.at[own], vbuf.at[pl.ds(partner_row, rows)], 7, partner)
    here = pl.ds(near_row, rows)
    there = pl.ds(shared_row, rows)
    share_k = remote(kbuf.at[here], kbuf.at[there], 8, partner)
    share_v = remote(vbuf.at[here], vbuf.at[there], 9, partner)

    small_copies = [
        pltpu.make_async_copy(src, dst, small_sem.at[j])
        for j, (src, dst) in enumerate((
            (gain_hbm, gain_ref), (halo_hbm, halo_ref), (counts_hbm, counts_ref),
            (mask_hbm, mask_ref),
        ))
    ]
    small_copies[0].start()
    tok_copies = []
    for r in range(4):
        part = pl.ds(r * chunk, chunk)
        copy = pltpu.make_async_copy(tokens_ref.at[part], tok.at[part], in_sem.at[r])
        copy.start()
        tok_copies.append(copy)
    for copy in small_copies[1:]:
        copy.start()
    w_copies = []
    for j in range(3):
        part = pl.ds(j * width, width)
        w_copies.append(
            pltpu.make_async_copy(wqkv_ref.at[:, part], wq.at[:, part], w_sem.at[j])
        )

    barrier = pltpu.get_barrier_semaphore()

    def greet(device):
        pl.semaphore_signal(barrier, inc=1, device_id=device, device_id_type=MESH)

    for device in (near, far_to, far_from, partner):
        greet(device)

    @pl.when(lat < nlat - 1)
    def _():
        greet(south)

    @pl.when(lat > 0)
    def _():
        greet(north)

    greeted = 4 + jnp.where(lat < nlat - 1, 1, 0) + jnp.where(lat > 0, 1, 0)

    small_copies[0].wait()
    gain = gain_ref[...]
    for r in range(4):
        part = pl.ds(r * chunk, chunk)
        tok_copies[r].wait()
        if r > 0:
            w_copies[r - 1].start()
        x = tok[part, :]
        average = jnp.mean(x, axis=-1, keepdims=True)
        centered = x - average
        variance = jnp.mean(centered * centered, axis=-1, keepdims=True)
        nown[part, :] = (centered * lax.rsqrt(variance + EPS) * gain).astype(bf16)
        if r == 1:
            pl.semaphore_wait(barrier, greeted)
            send_near[0].start()
    send_near[1].start()
    for copy in small_copies[1:]:
        copy.wait()

    to_south = halo_ref[jnp.minimum(lat + 1, nlat - 1), 0:1, :]
    to_north = halo_ref[jnp.maximum(lat - 1, 0), 1:2, :]
    slot = lax.broadcasted_iota(jnp.int32, (rows, halo), 0)
    for j, wanted in ((0, to_south), (1, to_north)):
        pick = jnp.where(slot == wanted, 1.0, 0.0).astype(bf16)
        hsend[j] = lax.dot_general(
            pick, nown[...], (((0,), (0,)), ((), ())), preferred_element_type=f32
        ).astype(bf16)

    @pl.when(lat == 0)
    def _():
        hrecv[pl.ds(0, halo), :] = jnp.zeros((halo, width), bf16)

    @pl.when(lat == nlat - 1)
    def _():
        hrecv[pl.ds(halo, halo), :] = jnp.zeros((halo, width), bf16)

    count = counts_ref[0]
    lane = lax.broadcasted_iota(jnp.int32, (1, 128), 1)
    low = lane < 64
    for r in range(4):
        feature = jnp.where(lane == LIVE_LANE, 1.0, 0.0)
        for c in range(5):
            hidden = (mask_ref[r, c].astype(f32) - 1.0) * BIG
            feature = feature + jnp.where(lane == c, hidden, 0.0)
        fq[pl.ds(r * chunk, chunk), :] = jnp.broadcast_to(feature, (chunk, 128)).astype(bf16)
    lanes = lax.broadcasted_iota(jnp.int32, (rows, 128), 1)
    position = lax.broadcasted_iota(jnp.int32, (rows, 128), 0)
    dead = jnp.where((lanes == LIVE_LANE) & (position >= count), -BIG, 0.0)
    for row, hops in (
        (0, 0), (partner_row, -side), (near_row, side), (far_row, 2 * side),
        (shared_row, -2 * side),
    ):
        fk[pl.ds(row, rows), :] = jnp.where(lanes == 2 + hops, 1.0, dead).astype(bf16)
    hlanes = lax.broadcasted_iota(jnp.int32, (2 * halo, 128), 1)
    hposition = lax.broadcasted_iota(jnp.int32, (2 * halo, 128), 0)
    gone = jnp.where(
        hposition < halo, jnp.where(lat == 0, -BIG, 0.0), jnp.where(lat == nlat - 1, -BIG, 0.0)
    )
    fk[pl.ds(halo_row, 2 * halo), :] = jnp.where(hlanes == LIVE_LANE, gone, 0.0).astype(bf16)

    low_b = jnp.where(low, 1.0, 0.0).astype(bf16)
    high_b = jnp.where(low, 0.0, 1.0).astype(bf16)

    tile = width // 2

    def project(src, column):
        return jnp.dot(src, wq[:, pl.ds(column, tile)], preferred_element_type=f32)

    def project_to(dst, row, src, column):
        for t in range(2):
            dst[pl.ds(row, src.shape[0]), pl.ds(t * tile, tile)] = project(
                src[...], column + t * tile
            ).astype(bf16)

    def att_copy(g):
        cols = pl.ds(pl.multiple_of(g * 256, 256), 256)
        return pltpu.make_async_copy(att.at[g], att_ref.at[:, cols], att_sem.at[g])

    def attend(row, keys, first=False, last=False, between=()):
        group = 4
        part = pl.ds(row, keys)
        steps = HEADS // group

        def columns(g, hh):
            return pl.ds(pl.multiple_of((g * (group // 2) + hh // 2) * 128, 128), 128)

        def scores(g, hh):
            return lax.dot_general(
                jnp.concatenate([q_ref[g * group + hh], fq[...]], axis=1),
                jnp.concatenate([kbuf[part, columns(g, hh)], fk[part, :]], axis=1),
                (((1,), (1,)), ((), ())), preferred_element_type=f32,
            )

        held = pl.ds(0, keys)
        sbuf[0, :, held] = scores(0, 0)

        def body(g, carry):
            for n, action in enumerate(between):
                pl.when(g == n + 1)(action)
            done = []
            for hh in range(group):
                h = g * group + hh
                odd = hh % 2
                cols = columns(g, hh)
                if hh + 1 < group:
                    later = scores(g, hh + 1)
                else:
                    later = scores(jnp.minimum(g + 1, steps - 1), 0)
                s = sbuf[odd, :, held]
                new = jnp.max(s, axis=1, keepdims=True)
                if first:
                    new = jnp.broadcast_to(new, (rows, 128))
                else:
                    old = m_ref[h]
                    new = jnp.maximum(old, new)
                p = jnp.exp(s - jnp.tile(new, (1, keys // 128))).astype(bf16)
                mine, other = (high_b, low_b) if odd else (low_b, high_b)
                o = jnp.dot(p, vbuf[part, cols] * mine + other, preferred_element_type=f32)
                if not first:
                    o = acc_ref[h] * jnp.exp(old - new) + o
                if last:
                    done.append(o)
                    if odd:
                        value = jnp.where(low, done[-2], done[-1])
                        total = pltpu.roll(jnp.where(low, done[-1], done[-2]), 64, axis=1)
                        att[g, :, (hh // 2) * 128:(hh // 2 + 1) * 128] = (value / total).astype(bf16)
                else:
                    acc_ref[h] = o
                    m_ref[h] = new
                sbuf[1 - odd, :, held] = later
            if last:
                att_copy(g).start()
            return carry

        lax.fori_loop(0, steps, body, 0)

    def start_rest():
        pl.when(lat < nlat - 1)(send_south.start)
        pl.when(lat > 0)(send_north.start)
        for copy in send_far:
            copy.start()

    def share_near():
        for copy in send_near:
            copy.wait_recv()
        project_to(kbuf, near_row, nrecv.at[0], width)
        share_k.start()
        project_to(vbuf, near_row, nrecv.at[0], 2 * width)
        share_v.start()

    w_copies[0].wait()
    for t in range(2):
        q = project(nown[...], t * tile) * 0.125
        for j in range(tile // 128):
            pair = q[:, j * 128:(j + 1) * 128]
            h = (t * (tile // 128) + j) * 2
            q_ref[h] = jnp.where(low, pair, 0.0).astype(bf16)
            q_ref[h + 1] = jnp.where(low, 0.0, pair).astype(bf16)
    w_copies[1].wait()
    project_to(kbuf, 0, nown, width)
    send_k.start()
    w_copies[2].wait()
    project_to(vbuf, 0, nown, 2 * width)
    send_v.start()

    send_k.wait_recv()
    send_v.wait_recv()
    attend(0, 2 * rows, first=True, between=(start_rest, share_near))

    share_k.wait_recv()
    share_v.wait_recv()
    attend(near_row, 2 * rows)

    pl.when(lat > 0)(send_south.wait_recv)
    pl.when(lat < nlat - 1)(send_north.wait_recv)
    project_to(kbuf, halo_row, hrecv, width)
    project_to(vbuf, halo_row, hrecv, 2 * width)
    for j, p in enumerate(halves):
        send_far[j].wait_recv()
        row = far_row + j * half
        project_to(kbuf, row, nrecv.at[1, p], width)
        project_to(vbuf, row, nrecv.at[1, p], 2 * width)
    attend(halo_row, 2 * halo + rows, last=True)
    for g in range(HEADS // 4):
        att_copy(g).wait()

    for copy in (*send_near, *send_far, send_k, send_v, share_k, share_v):
        copy.wait_send()

    pl.when(lat < nlat - 1)(send_south.wait_send)
    pl.when(lat > 0)(send_north.wait_send)


def output_kernel(
    counts_ref, att_hbm, tokens_hbm, wout_hbm, out_hbm, att, tok, wo, out, in_sem, w_sem, out_sem
):
    rows, width = tok.shape
    tiles = w_sem.shape[0]
    parts = [pl.ds(j * (width // tiles), width // tiles) for j in range(tiles)]
    att_copy = pltpu.make_async_copy(att_hbm, att, in_sem.at[tiles])
    att_copy.start()
    w_copies = []
    tok_copies = []
    for j, p in enumerate(parts):
        w_copies.append(pltpu.make_async_copy(wout_hbm.at[:, p], wo.at[:, p], w_sem.at[j]))
        w_copies[j].start()
        tok_copies.append(pltpu.make_async_copy(tokens_hbm.at[:, p], tok.at[:, p], in_sem.at[j]))
        tok_copies[j].start()
    live = lax.broadcasted_iota(jnp.int32, (rows, 1), 0) < counts_ref[0]
    att_copy.wait()
    out_copies = []
    for j, p in enumerate(parts):
        w_copies[j].wait()
        tok_copies[j].wait()
        y = tok[:, p] + jnp.dot(att[...], wo[:, p], preferred_element_type=f32)
        out[:, p] = jnp.where(live, y, 0.0)
        out_copies.append(pltpu.make_async_copy(out.at[:, p], out_hbm.at[:, p], out_sem.at[j]))
        out_copies[j].start()
    for copy in out_copies:
        copy.wait()


def on_device(tokens, norm_gain, qkv_weight, out_weight, band_counts, halo_rows, window_mask):
    rows, width = tokens.shape[2:]
    halo = halo_rows.shape[2]
    smem = pl.BlockSpec(memory_space=pltpu.SMEM)
    hbm = pl.BlockSpec(memory_space=pltpu.MemorySpace.HBM)
    dma = pltpu.SemaphoreType.DMA
    keys = 5 * rows + 2 * halo
    att = pl.pallas_call(
        attention_kernel,
        out_shape=jax.ShapeDtypeStruct((rows, width), bf16),
        in_specs=[hbm] * 6,
        out_specs=hbm,
        scratch_shapes=[
            pltpu.SMEM(band_counts.shape, jnp.int32),
            pltpu.SMEM(window_mask.shape[2:], jnp.int32),
            pltpu.VMEM((1, width), f32),
            pltpu.VMEM(halo_rows.shape, jnp.int32),
            pltpu.VMEM((rows, width), f32),
            pltpu.VMEM((width, 3 * width), bf16),
            pltpu.VMEM((rows, width), bf16),
            pltpu.VMEM((2, rows, width), bf16),
            pltpu.VMEM((2, halo, width), bf16),
            pltpu.VMEM((2 * halo, width), bf16),
            pltpu.VMEM((keys, width), bf16),
            pltpu.VMEM((keys, width), bf16),
            pltpu.VMEM((keys, 128), bf16),
            pltpu.VMEM((rows, 128), bf16),
            pltpu.VMEM((HEADS, rows, 128), bf16),
            pltpu.VMEM((HEADS, rows, 128), f32),
            pltpu.VMEM((HEADS, rows, 128), f32),
            pltpu.VMEM((HEADS // 4, rows, 256), bf16),
            pltpu.VMEM((2, rows, 2 * rows), f32),
            dma((4,)),
            dma((3,)),
            dma((4,)),
            dma((HEADS // 4,)),
            dma((10,)),
            dma((10,)),
        ],
        compiler_params=pltpu.CompilerParams(
            collective_id=0, has_side_effects=True, vmem_limit_bytes=67_000_000
        ),
        name="attention",
    )(
        band_counts, window_mask[0, 0], norm_gain[None, :], halo_rows,
        tokens[0, 0], qkv_weight,
    )
    out = pl.pallas_call(
        output_kernel,
        out_shape=jax.ShapeDtypeStruct((rows, width), f32),
        in_specs=[smem, hbm, hbm, hbm],
        out_specs=hbm,
        scratch_shapes=[
            pltpu.VMEM((rows, width), bf16),
            pltpu.VMEM((rows, width), f32),
            pltpu.VMEM((width, width), bf16),
            pltpu.VMEM((rows, width), f32),
            dma((3,)),
            dma((2,)),
            dma((2,)),
        ],
        compiler_params=pltpu.CompilerParams(vmem_limit_bytes=67_000_000),
        name="output",
    )(band_counts, att, tokens[0, 0], out_weight)
    return out[None, None]


def solution(mesh):
    in_specs = (
        P("lat", "lon", None, None),
        P(),
        P(),
        P(),
        P("lat"),
        P(),
        P("lat", "lon", None, None),
    )
    out_specs = P("lat", "lon", None, None)
    return jax.shard_map(
        on_device, mesh=mesh, in_specs=in_specs, out_specs=out_specs, check_vma=False
    )
```

```python
import jax
import jax.numpy as jnp
from jax import lax
from jax.experimental import pallas as pl
from jax.experimental.pallas import tpu as pltpu
from jax.sharding import PartitionSpec as P

HEADS = 16
EPS = 1e-05
BIG = 1e30
LIVE_LANE = 5
f32 = jnp.float32
bf16 = jnp.bfloat16
MESH = pl.DeviceIdType.MESH


def attention_kernel(
    counts_hbm, mask_hbm, gain_hbm, halo_hbm, tokens_ref, wqkv_ref,
    att_ref,
    counts_ref, mask_ref, gain_ref, halo_ref, tok, wq, nown, nrecv, hsend, hrecv, kbuf, vbuf, fk, fq, q_ref, m_ref, acc_ref, att, sbuf,
    in_sem, w_sem, small_sem, att_sem, send_sem, recv_sem,
):
    lat = lax.axis_index("lat")
    lon = lax.axis_index("lon")
    nlat = lax.axis_size("lat")
    nlon = lax.axis_size("lon")
    rows, width = tok.shape
    chunk = rows // 4
    half = rows // 2
    halo = hsend.shape[1]
    side = 2 * lax.rem(lon, 2) - 1

    def wrap(x):
        return lax.rem(x + nlon, nlon)

    partner_row = rows
    near_row = 2 * rows
    shared_row = near_row + rows
    halo_row = shared_row + rows
    far_row = halo_row + 2 * halo

    near = (lat, wrap(lon + side))
    far_to = (lat, wrap(lon - 2 * side))
    far_from = (lat, wrap(lon + 2 * side))
    partner = (lat, lon - side)
    south = (lax.rem(lat + 1, nlat), lon)
    north = (lax.rem(lat + nlat - 1, nlat), lon)

    def remote(src, dst, index, device):
        return pltpu.make_async_remote_copy(
            src_ref=src, dst_ref=dst, send_sem=send_sem.at[index], recv_sem=recv_sem.at[index],
            device_id=device, device_id_type=MESH,
        )

    halves = (pl.ds(0, half), pl.ds(half, half))
    send_near = [remote(nown.at[p], nrecv.at[0, p], j, near) for j, p in enumerate(halves)]
    send_far = [remote(nown.at[p], nrecv.at[1, p], 2 + j, far_to) for j, p in enumerate(halves)]
    send_south = remote(hsend.at[0], hrecv.at[pl.ds(0, halo)], 4, south)
    send_north = remote(hsend.at[1], hrecv.at[pl.ds(halo, halo)], 5, north)
    own = pl.ds(0, rows)
    send_k = remote(kbuf.at[own], kbuf.at[pl.ds(partner_row, rows)], 6, partner)
    send_v = remote(vbuf.at[own], vbuf.at[pl.ds(partner_row, rows)], 7, partner)
    here = pl.ds(near_row, rows)
    there = pl.ds(shared_row, rows)
    share_k = remote(kbuf.at[here], kbuf.at[there], 8, partner)
    share_v = remote(vbuf.at[here], vbuf.at[there], 9, partner)

    small_copies = [
        pltpu.make_async_copy(src, dst, small_sem.at[j])
        for j, (src, dst) in enumerate((
            (gain_hbm, gain_ref), (halo_hbm, halo_ref), (counts_hbm, counts_ref),
            (mask_hbm, mask_ref),
        ))
    ]
    small_copies[0].start()
    tok_copies = []
    for r in range(4):
        part = pl.ds(r * chunk, chunk)
        copy = pltpu.make_async_copy(tokens_ref.at[part], tok.at[part], in_sem.at[r])
        copy.start()
        tok_copies.append(copy)
    for copy in small_copies[1:]:
        copy.start()
    w_copies = []
    for j in range(3):
        part = pl.ds(j * width, width)
        w_copies.append(
            pltpu.make_async_copy(wqkv_ref.at[:, part], wq.at[:, part], w_sem.at[j])
        )

    barrier = pltpu.get_barrier_semaphore()

    def greet(device):
        pl.semaphore_signal(barrier, inc=1, device_id=device, device_id_type=MESH)

    for device in (near, far_to, far_from, partner):
        greet(device)

    @pl.when(lat < nlat - 1)
    def _():
        greet(south)

    @pl.when(lat > 0)
    def _():
        greet(north)

    greeted = 4 + jnp.where(lat < nlat - 1, 1, 0) + jnp.where(lat > 0, 1, 0)

    small_copies[0].wait()
    gain = gain_ref[...]
    for r in range(4):
        part = pl.ds(r * chunk, chunk)
        tok_copies[r].wait()
        if r > 0:
            w_copies[r - 1].start()
        x = tok[part, :]
        average = jnp.mean(x, axis=-1, keepdims=True)
        centered = x - average
        variance = jnp.mean(centered * centered, axis=-1, keepdims=True)
        nown[part, :] = (centered * lax.rsqrt(variance + EPS) * gain).astype(bf16)
        if r == 1:
            pl.semaphore_wait(barrier, greeted)
            send_near[0].start()
    send_near[1].start()
    for copy in small_copies[1:]:
        copy.wait()

    to_south = halo_ref[jnp.minimum(lat + 1, nlat - 1), 0:1, :]
    to_north = halo_ref[jnp.maximum(lat - 1, 0), 1:2, :]
    slot = lax.broadcasted_iota(jnp.int32, (rows, halo), 0)
    for j, wanted in ((0, to_south), (1, to_north)):
        pick = jnp.where(slot == wanted, 1.0, 0.0).astype(bf16)
        hsend[j] = lax.dot_general(
            pick, nown[...], (((0,), (0,)), ((), ())), preferred_element_type=f32
        ).astype(bf16)

    @pl.when(lat == 0)
    def _():
        hrecv[pl.ds(0, halo), :] = jnp.zeros((halo, width), bf16)

    @pl.when(lat == nlat - 1)
    def _():
        hrecv[pl.ds(halo, halo), :] = jnp.zeros((halo, width), bf16)

    count = counts_ref[0]
    lane = lax.broadcasted_iota(jnp.int32, (1, 128), 1)
    low = lane < 64
    for r in range(4):
        feature = jnp.where(lane == LIVE_LANE, 1.0, 0.0)
        for c in range(5):
            hidden = (mask_ref[r, c].astype(f32) - 1.0) * BIG
            feature = feature + jnp.where(lane == c, hidden, 0.0)
        fq[pl.ds(r * chunk, chunk), :] = jnp.broadcast_to(feature, (chunk, 128)).astype(bf16)
    lanes = lax.broadcasted_iota(jnp.int32, (rows, 128), 1)
    position = lax.broadcasted_iota(jnp.int32, (rows, 128), 0)
    dead = jnp.where((lanes == LIVE_LANE) & (position >= count), -BIG, 0.0)
    for row, hops in (
        (0, 0), (partner_row, -side), (near_row, side), (far_row, 2 * side),
        (shared_row, -2 * side),
    ):
        fk[pl.ds(row, rows), :] = jnp.where(lanes == 2 + hops, 1.0, dead).astype(bf16)
    hlanes = lax.broadcasted_iota(jnp.int32, (2 * halo, 128), 1)
    hposition = lax.broadcasted_iota(jnp.int32, (2 * halo, 128), 0)
    gone = jnp.where(
        hposition < halo, jnp.where(lat == 0, -BIG, 0.0), jnp.where(lat == nlat - 1, -BIG, 0.0)
    )
    fk[pl.ds(halo_row, 2 * halo), :] = jnp.where(hlanes == LIVE_LANE, gone, 0.0).astype(bf16)

    low_b = jnp.where(low, 1.0, 0.0).astype(bf16)
    high_b = jnp.where(low, 0.0, 1.0).astype(bf16)

    tile = width // 2

    def project(src, column):
        return jnp.dot(src, wq[:, pl.ds(column, tile)], preferred_element_type=f32)

    def project_to(dst, row, src, column):
        for t in range(2):
            dst[pl.ds(row, src.shape[0]), pl.ds(t * tile, tile)] = project(
                src[...], column + t * tile
            ).astype(bf16)

    def att_copy(g):
        cols = pl.ds(pl.multiple_of(g * 256, 256), 256)
        return pltpu.make_async_copy(att.at[g], att_ref.at[:, cols], att_sem.at[g])

    def attend(row, keys, first=False, last=False, between=()):
        group = 4
        part = pl.ds(row, keys)
        steps = HEADS // group

        def columns(g, hh):
            return pl.ds(pl.multiple_of((g * (group // 2) + hh // 2) * 128, 128), 128)

        def scores(g, hh):
            return lax.dot_general(
                jnp.concatenate([q_ref[g * group + hh], fq[...]], axis=1),
                jnp.concatenate([kbuf[part, columns(g, hh)], fk[part, :]], axis=1),
                (((1,), (1,)), ((), ())), preferred_element_type=f32,
            )

        held = pl.ds(0, keys)
        sbuf[0, :, held] = scores(0, 0)

        def body(g, carry):
            for n, action in enumerate(between):
                pl.when(g == n + 1)(action)
            done = []
            for hh in range(group):
                h = g * group + hh
                odd = hh % 2
                cols = columns(g, hh)
                if hh + 1 < group:
                    later = scores(g, hh + 1)
                else:
                    later = scores(jnp.minimum(g + 1, steps - 1), 0)
                s = sbuf[odd, :, held]
                new = jnp.max(s, axis=1, keepdims=True)
                if first:
                    new = jnp.broadcast_to(new, (rows, 128))
                else:
                    old = m_ref[h]
                    new = jnp.maximum(old, new)
                p = jnp.exp(s - jnp.tile(new, (1, keys // 128))).astype(bf16)
                mine, other = (high_b, low_b) if odd else (low_b, high_b)
                o = jnp.dot(p, vbuf[part, cols] * mine + other, preferred_element_type=f32)
                if not first:
                    o = acc_ref[h] * jnp.exp(old - new) + o
                if last:
                    done.append(o)
                    if odd:
                        value = jnp.where(low, done[-2], done[-1])
                        total = pltpu.roll(jnp.where(low, done[-1], done[-2]), 64, axis=1)
                        att[g, :, (hh // 2) * 128:(hh // 2 + 1) * 128] = (value / total).astype(bf16)
                else:
                    acc_ref[h] = o
                    m_ref[h] = new
                sbuf[1 - odd, :, held] = later
            if last:
                att_copy(g).start()
            return carry

        lax.fori_loop(0, steps, body, 0)

    def start_far():
        for copy in send_far:
            copy.start()

    def share_near():
        for copy in send_near:
            copy.wait_recv()
        project_to(kbuf, near_row, nrecv.at[0], width)
        share_k.start()
        project_to(vbuf, near_row, nrecv.at[0], 2 * width)
        share_v.start()

    w_copies[0].wait()
    for t in range(2):
        q = project(nown[...], t * tile) * 0.125
        for j in range(tile // 128):
            pair = q[:, j * 128:(j + 1) * 128]
            h = (t * (tile // 128) + j) * 2
            q_ref[h] = jnp.where(low, pair, 0.0).astype(bf16)
            q_ref[h + 1] = jnp.where(low, 0.0, pair).astype(bf16)
    w_copies[1].wait()
    project_to(kbuf, 0, nown, width)
    send_k.start()
    w_copies[2].wait()
    project_to(vbuf, 0, nown, 2 * width)
    send_v.start()

    send_k.wait_recv()
    send_v.wait_recv()
    attend(0, 2 * rows, first=True, between=(start_far, share_near))
    pl.when(lat < nlat - 1)(send_south.start)
    pl.when(lat > 0)(send_north.start)

    share_k.wait_recv()
    share_v.wait_recv()
    attend(near_row, 2 * rows)

    for j, p in enumerate(halves):
        send_far[j].wait_recv()
        row = far_row + j * half
        project_to(kbuf, row, nrecv.at[1, p], width)
        project_to(vbuf, row, nrecv.at[1, p], 2 * width)
    attend(far_row, rows)

    pl.when(lat > 0)(send_south.wait_recv)
    pl.when(lat < nlat - 1)(send_north.wait_recv)
    project_to(kbuf, halo_row, hrecv, width)
    project_to(vbuf, halo_row, hrecv, 2 * width)
    attend(halo_row, 2 * halo, last=True)
    for g in range(HEADS // 4):
        att_copy(g).wait()

    for copy in (*send_near, *send_far, send_k, send_v, share_k, share_v):
        copy.wait_send()

    pl.when(lat < nlat - 1)(send_south.wait_send)
    pl.when(lat > 0)(send_north.wait_send)


def output_kernel(
    counts_ref, att_hbm, tokens_hbm, wout_hbm, out_hbm, att, tok, wo, out, in_sem, w_sem, out_sem
):
    rows, width = tok.shape
    tiles = w_sem.shape[0]
    parts = [pl.ds(j * (width // tiles), width // tiles) for j in range(tiles)]
    att_copy = pltpu.make_async_copy(att_hbm, att, in_sem.at[tiles])
    att_copy.start()
    w_copies = []
    tok_copies = []
    for j, p in enumerate(parts):
        w_copies.append(pltpu.make_async_copy(wout_hbm.at[:, p], wo.at[:, p], w_sem.at[j]))
        w_copies[j].start()
        tok_copies.append(pltpu.make_async_copy(tokens_hbm.at[:, p], tok.at[:, p], in_sem.at[j]))
        tok_copies[j].start()
    live = lax.broadcasted_iota(jnp.int32, (rows, 1), 0) < counts_ref[0]
    att_copy.wait()
    out_copies = []
    for j, p in enumerate(parts):
        w_copies[j].wait()
        tok_copies[j].wait()
        y = tok[:, p] + jnp.dot(att[...], wo[:, p], preferred_element_type=f32)
        out[:, p] = jnp.where(live, y, 0.0)
        out_copies.append(pltpu.make_async_copy(out.at[:, p], out_hbm.at[:, p], out_sem.at[j]))
        out_copies[j].start()
    for copy in out_copies:
        copy.wait()


def on_device(tokens, norm_gain, qkv_weight, out_weight, band_counts, halo_rows, window_mask):
    rows, width = tokens.shape[2:]
    halo = halo_rows.shape[2]
    smem = pl.BlockSpec(memory_space=pltpu.SMEM)
    hbm = pl.BlockSpec(memory_space=pltpu.MemorySpace.HBM)
    dma = pltpu.SemaphoreType.DMA
    keys = 5 * rows + 2 * halo
    att = pl.pallas_call(
        attention_kernel,
        out_shape=jax.ShapeDtypeStruct((rows, width), bf16),
        in_specs=[hbm] * 6,
        out_specs=hbm,
        scratch_shapes=[
            pltpu.SMEM(band_counts.shape, jnp.int32),
            pltpu.SMEM(window_mask.shape[2:], jnp.int32),
            pltpu.VMEM((1, width), f32),
            pltpu.VMEM(halo_rows.shape, jnp.int32),
            pltpu.VMEM((rows, width), f32),
            pltpu.VMEM((width, 3 * width), bf16),
            pltpu.VMEM((rows, width), bf16),
            pltpu.VMEM((2, rows, width), bf16),
            pltpu.VMEM((2, halo, width), bf16),
            pltpu.VMEM((2 * halo, width), bf16),
            pltpu.VMEM((keys, width), bf16),
            pltpu.VMEM((keys, width), bf16),
            pltpu.VMEM((keys, 128), bf16),
            pltpu.VMEM((rows, 128), bf16),
            pltpu.VMEM((HEADS, rows, 128), bf16),
            pltpu.VMEM((HEADS, rows, 128), f32),
            pltpu.VMEM((HEADS, rows, 128), f32),
            pltpu.VMEM((HEADS // 4, rows, 256), bf16),
            pltpu.VMEM((2, rows, 2 * rows), f32),
            dma((4,)),
            dma((3,)),
            dma((4,)),
            dma((HEADS // 4,)),
            dma((10,)),
            dma((10,)),
        ],
        compiler_params=pltpu.CompilerParams(
            collective_id=0, has_side_effects=True, vmem_limit_bytes=67_000_000
        ),
        name="attention",
    )(
        band_counts, window_mask[0, 0], norm_gain[None, :], halo_rows,
        tokens[0, 0], qkv_weight,
    )
    out = pl.pallas_call(
        output_kernel,
        out_shape=jax.ShapeDtypeStruct((rows, width), f32),
        in_specs=[smem, hbm, hbm, hbm],
        out_specs=hbm,
        scratch_shapes=[
            pltpu.VMEM((rows, width), bf16),
            pltpu.VMEM((rows, width), f32),
            pltpu.VMEM((width, width), bf16),
            pltpu.VMEM((rows, width), f32),
            dma((3,)),
            dma((2,)),
            dma((2,)),
        ],
        compiler_params=pltpu.CompilerParams(vmem_limit_bytes=67_000_000),
        name="output",
    )(band_counts, att, tokens[0, 0], out_weight)
    return out[None, None]


def solution(mesh):
    in_specs = (
        P("lat", "lon", None, None),
        P(),
        P(),
        P(),
        P("lat"),
        P(),
        P("lat", "lon", None, None),
    )
    out_specs = P("lat", "lon", None, None)
    return jax.shard_map(
        on_device, mesh=mesh, in_specs=in_specs, out_specs=out_specs, check_vma=False
    )
```

```python
import jax
import jax.numpy as jnp
from jax import lax
from jax.experimental import pallas as pl
from jax.experimental.pallas import tpu as pltpu
from jax.sharding import PartitionSpec as P

HEADS = 16
EPS = 1e-05
BIG = 1e30
LIVE_LANE = 5
f32 = jnp.float32
bf16 = jnp.bfloat16
MESH = pl.DeviceIdType.MESH


def attention_kernel(
    counts_hbm, mask_hbm, gain_hbm, halo_hbm, tokens_ref, wqkv_ref,
    att_ref,
    counts_ref, mask_ref, gain_ref, halo_ref, tok, wq, nown, nrecv, hsend, hrecv, kbuf, vbuf, fk, fq, q_ref, m_ref, acc_ref, att, sbuf,
    in_sem, w_sem, small_sem, att_sem, send_sem, recv_sem,
):
    lat = lax.axis_index("lat")
    lon = lax.axis_index("lon")
    nlat = lax.axis_size("lat")
    nlon = lax.axis_size("lon")
    rows, width = tok.shape
    chunk = rows // 4
    half = rows // 2
    halo = hsend.shape[1]
    side = 2 * lax.rem(lon, 2) - 1

    def wrap(x):
        return lax.rem(x + nlon, nlon)

    partner_row = rows
    near_row = 2 * rows
    shared_row = near_row + rows
    halo_row = shared_row + rows
    far_row = halo_row + 2 * halo

    near = (lat, wrap(lon + side))
    far_to = (lat, wrap(lon - 2 * side))
    far_from = (lat, wrap(lon + 2 * side))
    partner = (lat, lon - side)
    south = (lax.rem(lat + 1, nlat), lon)
    north = (lax.rem(lat + nlat - 1, nlat), lon)

    def remote(src, dst, index, device):
        return pltpu.make_async_remote_copy(
            src_ref=src, dst_ref=dst, send_sem=send_sem.at[index], recv_sem=recv_sem.at[index],
            device_id=device, device_id_type=MESH,
        )

    halves = (pl.ds(0, half), pl.ds(half, half))
    send_near = [remote(nown.at[p], nrecv.at[0, p], j, near) for j, p in enumerate(halves)]
    send_far = [remote(nown.at[p], nrecv.at[1, p], 2 + j, far_to) for j, p in enumerate(halves)]
    send_south = remote(hsend.at[0], hrecv.at[pl.ds(0, halo)], 4, south)
    send_north = remote(hsend.at[1], hrecv.at[pl.ds(halo, halo)], 5, north)
    own = pl.ds(0, rows)
    send_k = remote(kbuf.at[own], kbuf.at[pl.ds(partner_row, rows)], 6, partner)
    send_v = remote(vbuf.at[own], vbuf.at[pl.ds(partner_row, rows)], 7, partner)
    here = pl.ds(near_row, rows)
    there = pl.ds(shared_row, rows)
    share_k = remote(kbuf.at[here], kbuf.at[there], 8, partner)
    share_v = remote(vbuf.at[here], vbuf.at[there], 9, partner)

    small_copies = [
        pltpu.make_async_copy(src, dst, small_sem.at[j])
        for j, (src, dst) in enumerate((
            (gain_hbm, gain_ref), (halo_hbm, halo_ref), (counts_hbm, counts_ref),
            (mask_hbm, mask_ref),
        ))
    ]
    small_copies[0].start()
    tok_copies = []
    for r in range(4):
        part = pl.ds(r * chunk, chunk)
        copy = pltpu.make_async_copy(tokens_ref.at[part], tok.at[part], in_sem.at[r])
        copy.start()
        tok_copies.append(copy)
    for copy in small_copies[1:]:
        copy.start()
    w_copies = []
    for j in range(3):
        part = pl.ds(j * width, width)
        w_copies.append(
            pltpu.make_async_copy(wqkv_ref.at[:, part], wq.at[:, part], w_sem.at[j])
        )

    barrier = pltpu.get_barrier_semaphore()

    def greet(device):
        pl.semaphore_signal(barrier, inc=1, device_id=device, device_id_type=MESH)

    for device in (near, far_to, far_from, partner):
        greet(device)

    @pl.when(lat < nlat - 1)
    def _():
        greet(south)

    @pl.when(lat > 0)
    def _():
        greet(north)

    greeted = 4 + jnp.where(lat < nlat - 1, 1, 0) + jnp.where(lat > 0, 1, 0)

    small_copies[0].wait()
    gain = gain_ref[...]
    for r in range(4):
        part = pl.ds(r * chunk, chunk)
        tok_copies[r].wait()
        if r > 0:
            w_copies[r - 1].start()
        x = tok[part, :]
        average = jnp.mean(x, axis=-1, keepdims=True)
        centered = x - average
        variance = jnp.mean(centered * centered, axis=-1, keepdims=True)
        nown[part, :] = (centered * lax.rsqrt(variance + EPS) * gain).astype(bf16)
        if r == 1:
            pl.semaphore_wait(barrier, greeted)
            send_near[0].start()
    send_near[1].start()
    for copy in small_copies[1:]:
        copy.wait()

    to_south = halo_ref[jnp.minimum(lat + 1, nlat - 1), 0:1, :]
    to_north = halo_ref[jnp.maximum(lat - 1, 0), 1:2, :]
    slot = lax.broadcasted_iota(jnp.int32, (rows, halo), 0)
    for j, wanted in ((0, to_south), (1, to_north)):
        pick = jnp.where(slot == wanted, 1.0, 0.0).astype(bf16)
        hsend[j] = lax.dot_general(
            pick, nown[...], (((0,), (0,)), ((), ())), preferred_element_type=f32
        ).astype(bf16)

    @pl.when(lat == 0)
    def _():
        hrecv[pl.ds(0, halo), :] = jnp.zeros((halo, width), bf16)

    @pl.when(lat == nlat - 1)
    def _():
        hrecv[pl.ds(halo, halo), :] = jnp.zeros((halo, width), bf16)

    count = counts_ref[0]
    lane = lax.broadcasted_iota(jnp.int32, (1, 128), 1)
    low = lane < 64
    for r in range(4):
        feature = jnp.where(lane == LIVE_LANE, 1.0, 0.0)
        for c in range(5):
            hidden = (mask_ref[r, c].astype(f32) - 1.0) * BIG
            feature = feature + jnp.where(lane == c, hidden, 0.0)
        fq[pl.ds(r * chunk, chunk), :] = jnp.broadcast_to(feature, (chunk, 128)).astype(bf16)
    lanes = lax.broadcasted_iota(jnp.int32, (rows, 128), 1)
    position = lax.broadcasted_iota(jnp.int32, (rows, 128), 0)
    dead = jnp.where((lanes == LIVE_LANE) & (position >= count), -BIG, 0.0)
    for row, hops in (
        (0, 0), (partner_row, -side), (near_row, side), (far_row, 2 * side),
        (shared_row, -2 * side),
    ):
        fk[pl.ds(row, rows), :] = jnp.where(lanes == 2 + hops, 1.0, dead).astype(bf16)
    hlanes = lax.broadcasted_iota(jnp.int32, (2 * halo, 128), 1)
    hposition = lax.broadcasted_iota(jnp.int32, (2 * halo, 128), 0)
    gone = jnp.where(
        hposition < halo, jnp.where(lat == 0, -BIG, 0.0), jnp.where(lat == nlat - 1, -BIG, 0.0)
    )
    fk[pl.ds(halo_row, 2 * halo), :] = jnp.where(hlanes == LIVE_LANE, gone, 0.0).astype(bf16)

    low_b = jnp.where(low, 1.0, 0.0).astype(bf16)
    high_b = jnp.where(low, 0.0, 1.0).astype(bf16)

    tile = width // 2

    def project(src, column):
        return jnp.dot(src, wq[:, pl.ds(column, tile)], preferred_element_type=f32)

    def project_to(dst, row, src, column):
        for t in range(2):
            dst[pl.ds(row, src.shape[0]), pl.ds(t * tile, tile)] = project(
                src[...], column + t * tile
            ).astype(bf16)

    def att_copy(g):
        cols = pl.ds(pl.multiple_of(g * 256, 256), 256)
        return pltpu.make_async_copy(att.at[g], att_ref.at[:, cols], att_sem.at[g])

    def attend(row, keys, first=False, last=False, between=(), group=4):
        part = pl.ds(row, keys)
        steps = HEADS // group

        def columns(g, hh):
            return pl.ds(pl.multiple_of((g * (group // 2) + hh // 2) * 128, 128), 128)

        def scores(g, hh):
            return lax.dot_general(
                jnp.concatenate([q_ref[g * group + hh], fq[...]], axis=1),
                jnp.concatenate([kbuf[part, columns(g, hh)], fk[part, :]], axis=1),
                (((1,), (1,)), ((), ())), preferred_element_type=f32,
            )

        held = pl.ds(0, keys)
        sbuf[0, :, held] = scores(0, 0)

        def body(g, carry):
            for n, action in enumerate(between):
                pl.when(g == n + 1)(action)
            done = []
            for hh in range(group):
                h = g * group + hh
                odd = hh % 2
                cols = columns(g, hh)
                if hh + 1 < group:
                    later = scores(g, hh + 1)
                else:
                    later = scores(jnp.minimum(g + 1, steps - 1), 0)
                s = sbuf[odd, :, held]
                new = jnp.max(s, axis=1, keepdims=True)
                if first:
                    new = jnp.broadcast_to(new, (rows, 128))
                else:
                    old = m_ref[h]
                    new = jnp.maximum(old, new)
                p = jnp.exp(s - jnp.tile(new, (1, keys // 128))).astype(bf16)
                mine, other = (high_b, low_b) if odd else (low_b, high_b)
                o = jnp.dot(p, vbuf[part, cols] * mine + other, preferred_element_type=f32)
                if not first:
                    o = acc_ref[h] * jnp.exp(old - new) + o
                if last:
                    done.append(o)
                    if odd:
                        value = jnp.where(low, done[-2], done[-1])
                        total = pltpu.roll(jnp.where(low, done[-1], done[-2]), 64, axis=1)
                        att[g, :, (hh // 2) * 128:(hh // 2 + 1) * 128] = (value / total).astype(bf16)
                else:
                    acc_ref[h] = o
                    m_ref[h] = new
                sbuf[1 - odd, :, held] = later
            if last:
                att_copy(g).start()
            return carry

        lax.fori_loop(0, steps, body, 0)

    def start_far():
        for copy in send_far:
            copy.start()

    def share_near():
        for copy in send_near:
            copy.wait_recv()
        project_to(kbuf, near_row, nrecv.at[0], width)
        share_k.start()
        project_to(vbuf, near_row, nrecv.at[0], 2 * width)
        share_v.start()

    w_copies[0].wait()
    for t in range(2):
        q = project(nown[...], t * tile) * 0.125
        for j in range(tile // 128):
            pair = q[:, j * 128:(j + 1) * 128]
            h = (t * (tile // 128) + j) * 2
            q_ref[h] = jnp.where(low, pair, 0.0).astype(bf16)
            q_ref[h + 1] = jnp.where(low, 0.0, pair).astype(bf16)
    w_copies[1].wait()
    project_to(kbuf, 0, nown, width)
    send_k.start()
    w_copies[2].wait()
    project_to(vbuf, 0, nown, 2 * width)
    send_v.start()

    send_k.wait_recv()
    send_v.wait_recv()
    attend(0, 2 * rows, first=True, between=(start_far, share_near))
    pl.when(lat < nlat - 1)(send_south.start)
    pl.when(lat > 0)(send_north.start)

    share_k.wait_recv()
    share_v.wait_recv()
    attend(near_row, 2 * rows, group=8)

    for j, p in enumerate(halves):
        send_far[j].wait_recv()
        row = far_row + j * half
        project_to(kbuf, row, nrecv.at[1, p], width)
        project_to(vbuf, row, nrecv.at[1, p], 2 * width)
    attend(far_row, rows, group=8)

    pl.when(lat > 0)(send_south.wait_recv)
    pl.when(lat < nlat - 1)(send_north.wait_recv)
    project_to(kbuf, halo_row, hrecv, width)
    project_to(vbuf, halo_row, hrecv, 2 * width)
    attend(halo_row, 2 * halo, last=True)
    for g in range(HEADS // 4):
        att_copy(g).wait()

    for copy in (*send_near, *send_far, send_k, send_v, share_k, share_v):
        copy.wait_send()

    pl.when(lat < nlat - 1)(send_south.wait_send)
    pl.when(lat > 0)(send_north.wait_send)


def output_kernel(
    counts_ref, att_hbm, tokens_hbm, wout_hbm, out_hbm, att, tok, wo, out, in_sem, w_sem, out_sem
):
    rows, width = tok.shape
    tiles = w_sem.shape[0]
    parts = [pl.ds(j * (width // tiles), width // tiles) for j in range(tiles)]
    att_copy = pltpu.make_async_copy(att_hbm, att, in_sem.at[tiles])
    att_copy.start()
    w_copies = []
    tok_copies = []
    for j, p in enumerate(parts):
        w_copies.append(pltpu.make_async_copy(wout_hbm.at[:, p], wo.at[:, p], w_sem.at[j]))
        w_copies[j].start()
        tok_copies.append(pltpu.make_async_copy(tokens_hbm.at[:, p], tok.at[:, p], in_sem.at[j]))
        tok_copies[j].start()
    live = lax.broadcasted_iota(jnp.int32, (rows, 1), 0) < counts_ref[0]
    att_copy.wait()
    out_copies = []
    for j, p in enumerate(parts):
        w_copies[j].wait()
        tok_copies[j].wait()
        y = tok[:, p] + jnp.dot(att[...], wo[:, p], preferred_element_type=f32)
        out[:, p] = jnp.where(live, y, 0.0)
        out_copies.append(pltpu.make_async_copy(out.at[:, p], out_hbm.at[:, p], out_sem.at[j]))
        out_copies[j].start()
    for copy in out_copies:
        copy.wait()


def on_device(tokens, norm_gain, qkv_weight, out_weight, band_counts, halo_rows, window_mask):
    rows, width = tokens.shape[2:]
    halo = halo_rows.shape[2]
    smem = pl.BlockSpec(memory_space=pltpu.SMEM)
    hbm = pl.BlockSpec(memory_space=pltpu.MemorySpace.HBM)
    dma = pltpu.SemaphoreType.DMA
    keys = 5 * rows + 2 * halo
    att = pl.pallas_call(
        attention_kernel,
        out_shape=jax.ShapeDtypeStruct((rows, width), bf16),
        in_specs=[hbm] * 6,
        out_specs=hbm,
        scratch_shapes=[
            pltpu.SMEM(band_counts.shape, jnp.int32),
            pltpu.SMEM(window_mask.shape[2:], jnp.int32),
            pltpu.VMEM((1, width), f32),
            pltpu.VMEM(halo_rows.shape, jnp.int32),
            pltpu.VMEM((rows, width), f32),
            pltpu.VMEM((width, 3 * width), bf16),
            pltpu.VMEM((rows, width), bf16),
            pltpu.VMEM((2, rows, width), bf16),
            pltpu.VMEM((2, halo, width), bf16),
            pltpu.VMEM((2 * halo, width), bf16),
            pltpu.VMEM((keys, width), bf16),
            pltpu.VMEM((keys, width), bf16),
            pltpu.VMEM((keys, 128), bf16),
            pltpu.VMEM((rows, 128), bf16),
            pltpu.VMEM((HEADS, rows, 128), bf16),
            pltpu.VMEM((HEADS, rows, 128), f32),
            pltpu.VMEM((HEADS, rows, 128), f32),
            pltpu.VMEM((HEADS // 4, rows, 256), bf16),
            pltpu.VMEM((2, rows, 2 * rows), f32),
            dma((4,)),
            dma((3,)),
            dma((4,)),
            dma((HEADS // 4,)),
            dma((10,)),
            dma((10,)),
        ],
        compiler_params=pltpu.CompilerParams(
            collective_id=0, has_side_effects=True, vmem_limit_bytes=67_000_000
        ),
        name="attention",
    )(
        band_counts, window_mask[0, 0], norm_gain[None, :], halo_rows,
        tokens[0, 0], qkv_weight,
    )
    out = pl.pallas_call(
        output_kernel,
        out_shape=jax.ShapeDtypeStruct((rows, width), f32),
        in_specs=[smem, hbm, hbm, hbm],
        out_specs=hbm,
        scratch_shapes=[
            pltpu.VMEM((rows, width), bf16),
            pltpu.VMEM((rows, width), f32),
            pltpu.VMEM((width, width), bf16),
            pltpu.VMEM((rows, width), f32),
            dma((3,)),
            dma((2,)),
            dma((2,)),
        ],
        compiler_params=pltpu.CompilerParams(vmem_limit_bytes=67_000_000),
        name="output",
    )(band_counts, att, tokens[0, 0], out_weight)
    return out[None, None]


def solution(mesh):
    in_specs = (
        P("lat", "lon", None, None),
        P(),
        P(),
        P(),
        P("lat"),
        P(),
        P("lat", "lon", None, None),
    )
    out_specs = P("lat", "lon", None, None)
    return jax.shard_map(
        on_device, mesh=mesh, in_specs=in_specs, out_specs=out_specs, check_vma=False
    )
```
